256 devices in a mesh: group: 8 (over z), tp: 32 (over y, x, core).
Axes of the slice: x: 4, y: 4, z: 8, core: 2. Of those that a mesh axis runs over, the one named last changes fastest.
Arguments:
- hidden_in: bfloat16 [512, 7168], P(('group', 'tp')), parts along dimension 0, may hold values from -4 to 4
- queries: bfloat16 [512, 32, 576], P(('group', 'tp')), parts along dimension 0, may hold values from -300 to 300
- cache: bfloat16 [512, 224, 576], P(('group', 'tp')), parts along dimension 0, may hold values from -4 to 4
- lengths: int32 [512], P(('group', 'tp')), parts along dimension 0, may hold values from 2 to 224, as said below
- w_uv: bfloat16 [32, 512, 128], P('tp'), may hold values from -0.5 to 0.5
- w_out: bfloat16 [4096, 7168], P('tp'), may hold values from -0.1875 to 0.1875
- norm_gain: bfloat16 [7168], replicated, may hold values from 0.5 to 1.5
- w_gate: bfloat16 [7168, 9216], P(None, 'tp'), may hold values from -0.0625 to 0.0625
- w_up: bfloat16 [7168, 9216], P(None, 'tp'), may hold values from -0.0625 to 0.0625
Outputs:
- attended: bfloat16 [512, 7168], P(('group', 'tp')), parts along dimension 0
- mlp_hidden: bfloat16 [512, 9216], P('group', 'tp'), parts along dimension 0
The draws below stay inside these ranges and needn't reach their ends.
There are 8 independent parts, one for each index of `group`. The reference program is written for one: setup_inputs(seed, part) draws one part's arguments, and reference() takes and returns one part's arrays. A program takes and returns all parts, laid end to end along the dimension named above; an argument that names none is the same for every part. Nothing has to cross between parts.
Inputs may be any that keep to these rules, and one draw needn't show every extreme that they name: `lengths`: in every draw some request has exactly 224 valid positions.
All inputs are finite; a program needn't handle non-finite values.
Results may differ from the reference program's by a relative error of at most 0.017.
Values may be sent and summed in bfloat16 or wider, within the bound.
A program may use at most 64 MiB of HBM per device.

```python
import math
import jax
import jax.numpy as jnp
from jax import lax

D = 7168
H = 32
LAT = 512
ROPE = 64
VD = 128
FF = 9216
REQ_DEV = 2
CACHE_LEN = 224
TOKENS = 64


def cache_values(key):
    base = jax.random.normal(jax.random.fold_in(key, 7), (TOKENS, CACHE_LEN, LAT + ROPE), jnp.float32)
    return jnp.clip(base, -4.0, 4.0)


def draw_cache(key, part):
    base = cache_values(key)
    return base.astype(jnp.bfloat16)


def draw_queries(key, part):
    drawn = jax.random.normal(jax.random.fold_in(key, 9), (TOKENS, H, LAT + ROPE), jnp.float32)
    drawn = jnp.clip(drawn, -6.0, 6.0)
    return drawn.astype(jnp.bfloat16)


def draw_lengths(key, part):
    block_total = TOKENS // REQ_DEV
    limits = jax.random.randint(jax.random.fold_in(key, 3), (block_total,), CACHE_LEN // 4, CACHE_LEN + 1)
    limit_rows = jnp.repeat(limits, REQ_DEV)
    drawn = jax.random.randint(jax.random.fold_in(key, 4), (TOKENS,), 2, limit_rows + 1)
    picked = jax.random.randint(jax.random.fold_in(key, 5), (), 0, TOKENS)
    return jnp.where(jnp.arange(TOKENS) == picked, CACHE_LEN, drawn).astype(jnp.int32)


def level_of(own_key, extent, split, least, high):
    def one(axis_at, parts):
        heights = jax.random.uniform(jax.random.fold_in(jax.random.fold_in(own_key, 6), axis_at), (parts,), jnp.float32, least / len(split), high / len(split))
        return jnp.repeat(jnp.exp(heights), extent[axis_at] // parts).reshape((-1,) + (1,) * (len(extent) - axis_at - 1))

    loudness = one(*split[0])
    for cut in split[1:]:
        loudness = loudness * one(*cut)
    return loudness


def noise(own_key, extent, width, bound, shards=(), kind=jnp.bfloat16):
    factor_of = level_of(own_key, extent, shards, -0.22, 0.18) if shards else 1.0
    values = jax.random.normal(own_key, extent, jnp.float32) * width * factor_of
    return jnp.minimum(jnp.maximum(values, -bound), bound).astype(kind)


def setup_inputs(seed: int = 0, part: int = 0) -> dict:
    splits = jax.random.split(jax.random.key(seed), 10)
    part_splits = jax.random.split(jax.random.fold_in(splits[9], part), 10)
    return {
        "hidden_in": noise(part_splits[0], (TOKENS, D), 0.5, 4.0, ((0, 32),)),
        "queries": draw_queries(jax.random.fold_in(jax.random.fold_in(splits[9], part), 71), part),
        "cache": draw_cache(jax.random.fold_in(jax.random.fold_in(splits[9], part), 71), part),
        "lengths": draw_lengths(jax.random.fold_in(jax.random.fold_in(splits[9], part), 71), part),
        "w_uv": noise(splits[4], (H, LAT, VD), (LAT // 4) ** -0.5, 0.5, ((0, 32),)),
        "w_out": noise(splits[5], (H * VD, D), (H * VD // 4) ** -0.5, 0.1875, ((0, 32),)),
        "norm_gain": jnp.clip(1.0 + 0.1 * jax.random.normal(splits[6], (D,), jnp.float32), 0.5, 1.5).astype(jnp.bfloat16),
        "w_gate": noise(splits[7], (D, FF), D ** -0.5, 0.0625, ((1, 32),)),
        "w_up": noise(splits[8], (D, FF), D ** -0.5, 0.0625, ((1, 32),)),
    }


def reference(hidden_in, queries, cache, lengths, w_uv, w_out, norm_gain, w_gate, w_up):
    score_scale = 1.0 / math.sqrt(VD + ROPE)

    def attend(items):
        query_row, cache_row, length_one = items
        scores = jnp.einsum('hk,jk->hj', query_row.astype(jnp.float32), cache_row.astype(jnp.float32)) * score_scale
        position = jnp.arange(CACHE_LEN, dtype=jnp.int32)
        visible = position[None, :] < length_one
        row_max = lax.optimization_barrier(jnp.max(jnp.where(visible, scores, -1e+30), axis=-1, keepdims=True))
        probs_full = jnp.exp(jnp.where(visible, scores - row_max, -1e+30))
        probs_low = probs_full.astype(jnp.bfloat16)
        summed = jnp.dot(probs_low, cache_row[:, :LAT], preferred_element_type=jnp.float32)
        return (summed / lax.optimization_barrier(jnp.sum(probs_full, axis=-1, keepdims=True))).astype(jnp.bfloat16)
    context = lax.map(attend, (queries, cache, lengths))
    values = jnp.einsum('thl,hlv->thv', context.astype(jnp.float32), w_uv.astype(jnp.float32)).astype(jnp.bfloat16)
    values = values.reshape(TOKENS, H * VD)
    residual = hidden_in.astype(jnp.float32) + jnp.dot(values, w_out, preferred_element_type=jnp.float32)
    attended = residual.astype(jnp.bfloat16)
    mean_square = lax.optimization_barrier(jnp.mean(residual * residual, axis=-1, keepdims=True))
    normed = (residual * lax.rsqrt(mean_square + 1e-06) * norm_gain.astype(jnp.float32)).astype(jnp.bfloat16)
    gate_part = jnp.dot(normed, w_gate, preferred_element_type=jnp.float32)
    up_part = jnp.dot(normed, w_up, preferred_element_type=jnp.float32)
    mlp_hidden = (jax.nn.silu(gate_part) * up_part).astype(jnp.bfloat16)
    return (attended, mlp_hidden)
```

```python
import math

import jax
import jax.numpy as jnp
from jax import lax
from jax.experimental import pallas as pl
from jax.experimental.pallas import tpu as pltpu
from jax.sharding import PartitionSpec as P

MESH = pl.DeviceIdType.MESH
SIDE = 4
CHIPS = SIDE * SIDE
LANES = 128
OFFSETS = sorted(
    ((dx, dy) for dx in range(SIDE) for dy in range(SIDE)),
    key=lambda o: -(min(o[0], SIDE - o[0]) + min(o[1], SIDE - o[1])),
)
COLUMN_ORDER = (2, 1, 3, 0)


def make_kernel(req, heads, latent, value, rotary, width, hidden, positions):
    tokens = req * 2 * CHIPS
    half = width // 2
    block = half // SIDE
    rows = tokens // SIDE
    score_scale = 1.0 / math.sqrt(value + rotary)
    pieces = latent // LANES

    def kernel(
        lengths_ref, hid_hbm, q_hbm, cache_hbm, wuv_hbm, wout_hbm, gain_ref, wg_hbm, wu_hbm,
        att_ref, mlp_ref,
        q_v, cache_v, wuv_v, w2_v, hid_v, wg_v, wu_v, send_perm, recv_perm,
        ctx_send, ctx_recv, part_v, red_v, x_v,
        in_sem, w2_sem, hid_sem, w2x_send, w2x_recv, hidx_send, hidx_recv, wuvx_send, wuvx_recv,
        ctx_ssem, ctx_rsem, red_ssem, red_rsem, all_ssem, all_rsem, fwd_ssem, fwd_rsem,
    ):
        group = lax.axis_index("group")
        me = lax.axis_index("tp")
        core = lax.rem(me, 2)
        other = 1 - core
        chip = me // 2
        cx = lax.rem(chip, SIDE)
        cy = chip // SIDE

        def chip_at(dx, dy):
            return lax.rem(cy + dy, SIDE) * SIDE + lax.rem(cx + dx, SIDE)

        def remote(src, dst, ssem, rsem, target):
            return pltpu.make_async_remote_copy(
                src_ref=src, dst_ref=dst, send_sem=ssem, recv_sem=rsem,
                device_id=(group, target), device_id_type=MESH,
            )

        partner = chip * 2 + other

        load_cache = pltpu.make_async_copy(cache_hbm, cache_v, in_sem.at[0])
        load_q = pltpu.make_async_copy(q_hbm, q_v, in_sem.at[1])
        load_cache.start()
        load_q.start()
        barrier = pltpu.get_barrier_semaphore()
        for dx, dy in OFFSETS:
            for dc in range(2):
                if (dx, dy, dc) != (0, 0, 0):
                    target = chip_at(dx, dy) * 2 + lax.rem(core + dc, 2)
                    pl.semaphore_signal(
                        barrier, inc=1, device_id=(group, target), device_id_type=MESH
                    )
        load_wuv = pltpu.make_async_copy(wuv_hbm.at[0], wuv_v.at[core], in_sem.at[2])
        load_wuv.start()

        def columns(which, b):
            return pl.ds(pl.multiple_of(which * half + b * block, LANES), block)

        loads_w2 = []
        loads_hid = []
        for b in range(SIDE):
            loads_w2.append(
                pltpu.make_async_copy(
                    wout_hbm.at[:, columns(core, b)], w2_v.at[b, core], w2_sem.at[b]
                )
            )
            loads_hid.append(
                pltpu.make_async_copy(
                    hid_hbm.at[:, columns(core, b)], hid_v.at[b, core], hid_sem.at[b]
                )
            )
        for copy in loads_w2 + loads_hid:
            copy.start()
        load_wg = pltpu.make_async_copy(wg_hbm, wg_v, in_sem.at[3])
        load_wu = pltpu.make_async_copy(wu_hbm, wu_v, in_sem.at[4])
        load_wg.start()
        load_wu.start()

        size = CHIPS * 16
        row = lax.broadcasted_iota(jnp.int32, (size, size), 0)
        col = lax.broadcasted_iota(jnp.int32, (size, size), 1)
        to = row // 16
        item = row % 16
        src_row = ((item % 2) * pieces + (item // 2) % pieces) * heads + to * 2 + item // (2 * pieces)
        send_perm[...] = (col == src_row).astype(jnp.bfloat16)
        tok = row % 32
        src_row = (tok // 2) * 16 + (row // 32) * 2 + tok % 2
        recv_perm[...] = (col == src_row).astype(jnp.bfloat16)

        load_cache.wait()
        load_q.wait()
        position = lax.broadcasted_iota(jnp.int32, (heads, positions), 1)
        parts = []
        for r in range(req):
            keys = cache_v[r]
            scores = (
                lax.dot_general(
                    q_v[r], keys, (((1,), (1,)), ((), ())), preferred_element_type=jnp.float32
                )
                * score_scale
            )
            visible = position < lengths_ref[r]
            top = jnp.max(jnp.where(visible, scores, -1e30), axis=-1, keepdims=True)
            probs = jnp.exp(jnp.where(visible, scores - top, -1e30))
            total = jnp.sum(probs, axis=-1, keepdims=True)
            summed = jnp.dot(
                probs.astype(jnp.bfloat16), keys[:, :latent], preferred_element_type=jnp.float32
            )
            ctx = (summed / total).astype(jnp.bfloat16)
            for p in range(pieces):
                parts.append(ctx[:, p * LANES : (p + 1) * LANES])
        ctx_send[...] = (
            jnp.dot(
                send_perm[...], jnp.concatenate(parts, axis=0), preferred_element_type=jnp.float32
            )
            .astype(jnp.bfloat16)
            .reshape(CHIPS, 16, LANES)
        )

        pl.semaphore_wait(barrier, 2 * CHIPS - 1)

        sends = []
        for dx, dy in OFFSETS:
            for dc in range(2):
                if (dx, dy, dc) != (0, 0, 0):
                    to_chip = chip_at(dx, dy)
                    target = to_chip * 2 + lax.rem(core + dc, 2)
                    copy = remote(
                        ctx_send.at[to_chip], ctx_recv.at[me],
                        ctx_ssem.at[target], ctx_rsem.at[me], target,
                    )
                    copy.start()
                    sends.append(copy)
        trade_wuv = remote(
            wuv_hbm.at[0], wuv_v.at[core], wuvx_send.at[0], wuvx_recv.at[0], partner
        )
        trade_wuv.start()
        trade_w2 = []
        trade_hid = []
        for b in range(SIDE):
            trade_w2.append(
                remote(
                    wout_hbm.at[:, columns(other, b)], w2_v.at[b, core],
                    w2x_send.at[b], w2x_recv.at[b], partner,
                )
            )
            trade_hid.append(
                remote(
                    hid_hbm.at[:, columns(other, b)], hid_v.at[b, core],
                    hidx_send.at[b], hidx_recv.at[b], partner,
                )
            )
        for copy in trade_w2 + trade_hid:
            copy.start()
        ctx_recv[me] = ctx_send[chip]

        for copy in [load_wuv] + loads_w2 + loads_hid:
            copy.wait()
        trade_wuv.wait_recv()
        for copy in trade_w2 + trade_hid:
            copy.wait_recv()
        for dx, dy in reversed(OFFSETS):
            for dc in range(2):
                if (dx, dy, dc) != (0, 0, 0):
                    source = chip_at(dx, dy) * 2 + lax.rem(core + dc, 2)
                    remote(
                        ctx_send.at[0], ctx_recv.at[source],
                        ctx_ssem.at[source], ctx_rsem.at[source], source,
                    ).wait_recv()

        got = ctx_recv[...].reshape(2, size, LANES)
        ordered = [
            jnp.dot(recv_perm[...], got[k], preferred_element_type=jnp.float32).astype(jnp.bfloat16)
            for k in range(2)
        ]
        vals = []
        for h in range(2):
            ctx = jnp.concatenate(
                [
                    jnp.concatenate(
                        [o[(h * pieces + p) * 32 : (h * pieces + p + 1) * 32] for p in range(pieces)],
                        axis=1,
                    )
                    for o in ordered
                ],
                axis=0,
            )
            vals.append(
                jnp.dot(ctx, wuv_v[h], preferred_element_type=jnp.float32).astype(jnp.bfloat16)
            )
        vals = jnp.concatenate(vals, axis=1)

        token = lax.broadcasted_iota(jnp.int32, (tokens, block), 0)
        for dx in COLUMN_ORDER:
            b = lax.rem(cx + dx, SIDE)
            part = jnp.dot(
                vals, w2_v[b].reshape(2 * value, block), preferred_element_type=jnp.float32
            )
            own = hid_v[b].astype(jnp.float32)
            for h in range(2):
                for r in range(req):
                    part = part + jnp.where(
                        token == chip * (2 * req) + h * req + r, own[h, r : r + 1, :], 0.0
                    )
            part_v[b] = part.astype(jnp.bfloat16).reshape(SIDE, rows, block)
            for dy in COLUMN_ORDER:
                if (dx, dy) != (0, 0):
                    to_chip = chip_at(dx, dy)
                    copy = remote(
                        part_v.at[b, lax.rem(cy + dy, SIDE)], red_v.at[chip],
                        red_ssem.at[to_chip], red_rsem.at[chip], to_chip * 2 + core,
                    )
                    copy.start()
                    sends.append(copy)
        red_v[chip] = part_v[cx, cy]
        for dx, dy in reversed(OFFSETS):
            if (dx, dy) != (0, 0):
                source = chip_at(dx, dy)
                remote(
                    part_v.at[0, 0], red_v.at[source],
                    red_ssem.at[source], red_rsem.at[source], source * 2 + core,
                ).wait_recv()
        total = red_v[0].astype(jnp.float32)
        for k in range(1, CHIPS):
            total = total + red_v[k].astype(jnp.float32)
        x_v[core, cx, cy] = total.astype(jnp.bfloat16)

        for dx, dy in OFFSETS:
            if (dx, dy) != (0, 0):
                to_chip = chip_at(dx, dy)
                copy = remote(
                    x_v.at[core, cx, cy], x_v.at[core, cx, cy],
                    all_ssem.at[to_chip], all_rsem.at[chip], to_chip * 2 + core,
                )
                copy.start()
                sends.append(copy)

        load_wg.wait()
        load_wu.wait()
        gate = jnp.zeros((tokens, hidden), jnp.float32)
        up = jnp.zeros((tokens, hidden), jnp.float32)
        square = jnp.zeros((tokens, 1), jnp.float32)

        def multiply(which, b, carry):
            gate, up, square = carry
            x = x_v[which, b].reshape(tokens, block).astype(jnp.float32)
            square = square + jnp.sum(x * x, axis=-1, keepdims=True)
            x = (x * gain_ref[which * SIDE + b].astype(jnp.float32)).astype(jnp.bfloat16)
            span = pl.ds(pl.multiple_of(which * half + b * block, block), block)
            gate = gate + jnp.dot(x, wg_v[span, :], preferred_element_type=jnp.float32)
            up = up + jnp.dot(x, wu_v[span, :], preferred_element_type=jnp.float32)
            return (gate, up, square)

        carry = (gate, up, square)
        forwards = []
        for dx in reversed(COLUMN_ORDER):
            b = lax.rem(cx + dx, SIDE)
            for dy in reversed(COLUMN_ORDER):
                if (dx, dy) != (0, 0):
                    source = chip_at(dx, dy)
                    a = lax.rem(cy + dy, SIDE)
                    remote(
                        x_v.at[core, b, a], x_v.at[core, b, a],
                        all_ssem.at[source], all_rsem.at[source], source * 2 + core,
                    ).wait_recv()
            copy = remote(
                x_v.at[core, b], x_v.at[core, b], fwd_ssem.at[b], fwd_rsem.at[b], partner
            )
            copy.start()
            sends.append(copy)
            carry = multiply(core, b, carry)
        for dx in reversed(COLUMN_ORDER):
            b = lax.rem(cx + dx, SIDE)
            remote(
                x_v.at[other, b], x_v.at[other, b], fwd_ssem.at[b], fwd_rsem.at[b], partner
            ).wait_recv()
            carry = multiply(other, b, carry)
        gate, up, square = carry
        scale = lax.rsqrt(square / width + 1e-6)
        gate = gate * scale
        up = up * scale
        mlp_ref[...] = (gate / (1.0 + jnp.exp(-gate)) * up).astype(jnp.bfloat16)

        first = lax.rem(chip, SIDE) * (2 * req) + core * req
        line = lax.broadcasted_iota(jnp.int32, (rows, block), 0)
        for which in range(2):
            for b in range(SIDE):
                x = x_v[which, b, cy].astype(jnp.float32)
                picked = jnp.concatenate(
                    [
                        jnp.sum(jnp.where(line == first + r, x, 0.0), axis=0, keepdims=True)
                        for r in range(req)
                    ],
                    axis=0,
                )
                at = which * half + b * block
                att_ref[:, at : at + block] = picked.astype(jnp.bfloat16)

        for copy in sends + [trade_wuv] + trade_w2 + trade_hid:
            copy.wait_send()

    return kernel


def per_device(hidden_in, queries, cache, lengths, w_uv, w_out, norm_gain, w_gate, w_up):
    req, heads, depth = queries.shape
    positions = cache.shape[1]
    latent, value = w_uv.shape[1:]
    width, hidden = w_gate.shape
    rotary = depth - latent
    tokens = req * 2 * CHIPS
    half = width // 2
    block = half // SIDE
    rows = tokens // SIDE
    size = CHIPS * 16
    bf16 = jnp.bfloat16
    dma = pltpu.SemaphoreType.DMA
    hbm = pl.BlockSpec(memory_space=pl.ANY)
    vmem = pl.BlockSpec(memory_space=pltpu.VMEM)
    return pl.pallas_call(
        make_kernel(req, heads, latent, value, rotary, width, hidden, positions),
        out_shape=(
            jax.ShapeDtypeStruct((req, width), bf16),
            jax.ShapeDtypeStruct((tokens, hidden), bf16),
        ),
        in_specs=[pl.BlockSpec(memory_space=pltpu.SMEM), hbm, hbm, hbm, hbm, hbm, vmem, hbm, hbm],
        out_specs=(vmem, vmem),
        scratch_shapes=[
            pltpu.VMEM((req, heads, depth), bf16),
            pltpu.VMEM((req, positions, depth), bf16),
            pltpu.VMEM((2, latent, value), bf16),
            pltpu.VMEM((SIDE, 2, value, block), bf16),
            pltpu.VMEM((SIDE, 2, req, block), bf16),
            pltpu.VMEM((width, hidden), bf16),
            pltpu.VMEM((width, hidden), bf16),
            pltpu.VMEM((size, size), bf16),
            pltpu.VMEM((size, size), bf16),
            pltpu.VMEM((CHIPS, 16, LANES), bf16),
            pltpu.VMEM((2 * CHIPS, 16, LANES), bf16),
            pltpu.VMEM((SIDE, SIDE, rows, block), bf16),
            pltpu.VMEM((CHIPS, rows, block), bf16),
            pltpu.VMEM((2, SIDE, SIDE, rows, block), bf16),
            dma((5,)),
            dma((SIDE,)),
            dma((SIDE,)),
            dma((SIDE,)),
            dma((SIDE,)),
            dma((SIDE,)),
            dma((SIDE,)),
            dma((1,)),
            dma((1,)),
            dma((2 * CHIPS,)),
            dma((2 * CHIPS,)),
            dma((CHIPS,)),
            dma((CHIPS,)),
            dma((CHIPS,)),
            dma((CHIPS,)),
            dma((SIDE,)),
            dma((SIDE,)),
        ],
        compiler_params=pltpu.CompilerParams(
            collective_id=0, has_side_effects=True, vmem_limit_bytes=40 * 1024 * 1024
        ),
    )(
        lengths, hidden_in, queries, cache, w_uv, w_out,
        norm_gain.reshape(2 * SIDE, 1, block), w_gate, w_up,
    )


def solution(mesh):
    in_specs = (
        P(("group", "tp"), None),
        P(("group", "tp"), None, None),
        P(("group", "tp"), None, None),
        P(("group", "tp")),
        P("tp", None, None),
        P("tp", None),
        P(),
        P(None, "tp"),
        P(None, "tp"),
    )
    out_specs = (P(("group", "tp"), None), P("group", "tp"))
    return jax.shard_map(
        per_device, mesh=mesh, in_specs=in_specs, out_specs=out_specs, check_vma=False
    )
```

```python
import math

import jax
import jax.numpy as jnp
from jax import lax
from jax.experimental import pallas as pl
from jax.experimental.pallas import tpu as pltpu
from jax.sharding import PartitionSpec as P

MESH = pl.DeviceIdType.MESH
SIDE = 4
CHIPS = SIDE * SIDE
LANES = 128
OFFSETS = sorted(
    ((dx, dy) for dx in range(SIDE) for dy in range(SIDE)),
    key=lambda o: -(min(o[0], SIDE - o[0]) + min(o[1], SIDE - o[1])),
)
COLUMN_ORDER = (2, 1, 3, 0)


def make_kernel(req, heads, latent, value, rotary, width, hidden, positions):
    tokens = req * 2 * CHIPS
    half = width // 2
    block = half // SIDE
    rows = tokens // SIDE
    score_scale = 1.0 / math.sqrt(value + rotary)
    pieces = latent // LANES

    def kernel(
        lengths_hbm, hid_hbm, q_hbm, cache_hbm, wuv_hbm, wout_hbm, gain_hbm, wg_hbm, wu_hbm,
        att_ref, mlp_ref,
        lengths_s, q_v, cache_v, wuv_v, w2_v, hid_v, gain_v, gain_f, mlp_v, send_perm, recv_perm,
        ctx_send, ctx_recv, part_v, red_v, x_v,
        in_sem, w2_sem, hid_sem, mlp_sem, w2x_send, w2x_recv, hidx_send, hidx_recv, wuvx_send, wuvx_recv,
        ctx_ssem, ctx_rsem, red_ssem, red_rsem, all_ssem, all_rsem, fwd_ssem, fwd_rsem,
    ):
        group = lax.axis_index("group")
        me = lax.axis_index("tp")
        core = lax.rem(me, 2)
        other = 1 - core
        chip = me // 2
        cx = lax.rem(chip, SIDE)
        cy = chip // SIDE

        def chip_at(dx, dy):
            return lax.rem(cy + dy, SIDE) * SIDE + lax.rem(cx + dx, SIDE)

        def remote(src, dst, ssem, rsem, target):
            return pltpu.make_async_remote_copy(
                src_ref=src, dst_ref=dst, send_sem=ssem, recv_sem=rsem,
                device_id=(group, target), device_id_type=MESH,
            )

        partner = chip * 2 + other

        load_cache = pltpu.make_async_copy(cache_hbm, cache_v, in_sem.at[0])
        load_q = pltpu.make_async_copy(q_hbm, q_v, in_sem.at[1])
        load_lengths = pltpu.make_async_copy(lengths_hbm, lengths_s, in_sem.at[3])
        load_gain = pltpu.make_async_copy(gain_hbm, gain_v, in_sem.at[4])
        load_cache.start()
        load_q.start()
        load_lengths.start()
        load_gain.start()
        barrier = pltpu.get_barrier_semaphore()
        for dx, dy in OFFSETS:
            for dc in range(2):
                if (dx, dy, dc) != (0, 0, 0):
                    target = chip_at(dx, dy) * 2 + lax.rem(core + dc, 2)
                    pl.semaphore_signal(
                        barrier, inc=1, device_id=(group, target), device_id_type=MESH
                    )
        load_wuv = pltpu.make_async_copy(wuv_hbm.at[0], wuv_v.at[core], in_sem.at[2])
        load_wuv.start()

        def columns(which, b):
            return pl.ds(pl.multiple_of(which * half + b * block, LANES), block)

        loads_w2 = []
        loads_hid = []
        for b in range(SIDE):
            loads_w2.append(
                pltpu.make_async_copy(
                    wout_hbm.at[:, columns(core, b)], w2_v.at[b, core], w2_sem.at[b]
                )
            )
            loads_hid.append(
                pltpu.make_async_copy(
                    hid_hbm.at[:, columns(core, b)], hid_v.at[b, core], hid_sem.at[b]
                )
            )
        for copy in loads_w2 + loads_hid:
            copy.start()
        loads_mlp = []
        for k in range(2 * SIDE):
            for i, weight in enumerate((wg_hbm, wu_hbm)):
                loads_mlp.append(
                    pltpu.make_async_copy(
                        weight.at[:, pl.ds(k * block, block)],
                        mlp_v.at[k, pl.ds(i * hidden, hidden)],
                        mlp_sem.at[2 * k + i],
                    )
                )
        for copy in loads_mlp:
            copy.start()

        size = CHIPS * 16
        row = lax.broadcasted_iota(jnp.int32, (size, size), 0)
        col = lax.broadcasted_iota(jnp.int32, (size, size), 1)
        to = row // 16
        item = row % 16
        src_row = ((item % 2) * pieces + (item // 2) % pieces) * heads + to * 2 + item // (2 * pieces)
        send_perm[...] = (col == src_row).astype(jnp.bfloat16)
        tok = row % 32
        src_row = (tok // 2) * 16 + (row // 32) * 2 + tok % 2
        recv_perm[...] = (col == src_row).astype(jnp.bfloat16)

        load_lengths.wait()
        load_cache.wait()
        load_q.wait()
        position = lax.broadcasted_iota(jnp.int32, (heads, positions), 1)
        parts = []
        for r in range(req):
            keys = cache_v[r]
            scores = (
                lax.dot_general(
                    q_v[r], keys, (((1,), (1,)), ((), ())), preferred_element_type=jnp.float32
                )
                * score_scale
            )
            visible = position < lengths_s[r]
            top = jnp.max(jnp.where(visible, scores, -1e30), axis=-1, keepdims=True)
            probs = jnp.exp(jnp.where(visible, scores - top, -1e30))
            total = jnp.sum(probs, axis=-1, keepdims=True)
            summed = jnp.dot(
                probs.astype(jnp.bfloat16), keys[:, :latent], preferred_element_type=jnp.float32
            )
            ctx = (summed / total).astype(jnp.bfloat16)
            for p in range(pieces):
                parts.append(ctx[:, p * LANES : (p + 1) * LANES])
        ctx_send[...] = (
            jnp.dot(
                send_perm[...], jnp.concatenate(parts, axis=0), preferred_element_type=jnp.float32
            )
            .astype(jnp.bfloat16)
            .reshape(CHIPS, 16, LANES)
        )

        pl.semaphore_wait(barrier, 2 * CHIPS - 1)

        sends = []
        for dx, dy in OFFSETS:
            for dc in range(2):
                if (dx, dy, dc) != (0, 0, 0):
                    to_chip = chip_at(dx, dy)
                    target = to_chip * 2 + lax.rem(core + dc, 2)
                    copy = remote(
                        ctx_send.at[to_chip], ctx_recv.at[me],
                        ctx_ssem.at[target], ctx_rsem.at[me], target,
                    )
                    copy.start()
                    sends.append(copy)
        trade_wuv = remote(
            wuv_hbm.at[0], wuv_v.at[core], wuvx_send.at[0], wuvx_recv.at[0], partner
        )
        trade_wuv.start()
        trade_w2 = []
        trade_hid = []
        for b in range(SIDE):
            trade_w2.append(
                remote(
                    wout_hbm.at[:, columns(other, b)], w2_v.at[b, core],
                    w2x_send.at[b], w2x_recv.at[b], partner,
                )
            )
            trade_hid.append(
                remote(
                    hid_hbm.at[:, columns(other, b)], hid_v.at[b, core],
                    hidx_send.at[b], hidx_recv.at[b], partner,
                )
            )
        for copy in trade_w2 + trade_hid:
            copy.start()
        ctx_recv[me] = ctx_send[chip]

        for copy in [load_wuv] + loads_w2 + loads_hid:
            copy.wait()
        trade_wuv.wait_recv()
        for copy in trade_w2 + trade_hid:
            copy.wait_recv()
        for dx, dy in reversed(OFFSETS):
            for dc in range(2):
                if (dx, dy, dc) != (0, 0, 0):
                    source = chip_at(dx, dy) * 2 + lax.rem(core + dc, 2)
                    remote(
                        ctx_send.at[0], ctx_recv.at[source],
                        ctx_ssem.at[source], ctx_rsem.at[source], source,
                    ).wait_recv()

        got = ctx_recv[...].reshape(2, size, LANES)
        ordered = [
            jnp.dot(recv_perm[...], got[k], preferred_element_type=jnp.float32).astype(jnp.bfloat16)
            for k in range(2)
        ]
        vals = []
        for h in range(2):
            ctx = jnp.concatenate(
                [
                    jnp.concatenate(
                        [o[(h * pieces + p) * 32 : (h * pieces + p + 1) * 32] for p in range(pieces)],
                        axis=1,
                    )
                    for o in ordered
                ],
                axis=0,
            )
            vals.append(
                jnp.dot(ctx, wuv_v[h], preferred_element_type=jnp.float32).astype(jnp.bfloat16)
            )
        vals = jnp.concatenate(vals, axis=1)

        token = lax.broadcasted_iota(jnp.int32, (tokens, block), 0)
        for dx in COLUMN_ORDER:
            b = lax.rem(cx + dx, SIDE)
            part = jnp.dot(
                vals, w2_v[b].reshape(2 * value, block), preferred_element_type=jnp.float32
            )
            own = hid_v[b].astype(jnp.float32)
            for h in range(2):
                for r in range(req):
                    part = part + jnp.where(
                        token == chip * (2 * req) + h * req + r, own[h, r : r + 1, :], 0.0
                    )
            part_v[b] = part.astype(jnp.bfloat16).reshape(SIDE, rows, block)
            for dy in COLUMN_ORDER:
                if (dx, dy) != (0, 0):
                    to_chip = chip_at(dx, dy)
                    copy = remote(
                        part_v.at[b, lax.rem(cy + dy, SIDE)], red_v.at[chip],
                        red_ssem.at[to_chip], red_rsem.at[chip], to_chip * 2 + core,
                    )
                    copy.start()
                    sends.append(copy)
        red_v[chip] = part_v[cx, cy]
        for dx, dy in reversed(OFFSETS):
            if (dx, dy) != (0, 0):
                source = chip_at(dx, dy)
                remote(
                    part_v.at[0, 0], red_v.at[source],
                    red_ssem.at[source], red_rsem.at[source], source * 2 + core,
                ).wait_recv()
        total = red_v[0].astype(jnp.float32)
        for k in range(1, CHIPS):
            total = total + red_v[k].astype(jnp.float32)
        x_v[core, cx, cy] = total.astype(jnp.bfloat16)

        for dx, dy in OFFSETS:
            if (dx, dy) != (0, 0):
                to_chip = chip_at(dx, dy)
                copy = remote(
                    x_v.at[core, cx, cy], x_v.at[core, cx, cy],
                    all_ssem.at[to_chip], all_rsem.at[chip], to_chip * 2 + core,
                )
                copy.start()
                sends.append(copy)

        load_gain.wait()
        gains = gain_v[...].astype(jnp.float32)
        for k in range(2 * SIDE):
            for i in range(block // LANES):
                at = k * (block // LANES) + i
                gain_f[k, 0:1, i * LANES : (i + 1) * LANES] = gains[at : at + 1, :]
        for copy in loads_mlp:
            copy.wait()
        both = jnp.zeros((tokens, 2 * hidden), jnp.float32)
        square = jnp.zeros((tokens, 1), jnp.float32)

        def multiply(which, b, carry):
            both, square = carry
            k = which * SIDE + b
            x = x_v[which, b].reshape(tokens, block).astype(jnp.float32)
            square = square + jnp.sum(x * x, axis=-1, keepdims=True)
            x = (x * gain_f[k]).astype(jnp.bfloat16)
            both = both + lax.dot_general(
                x, mlp_v[k], (((1,), (1,)), ((), ())), preferred_element_type=jnp.float32
            )
            return (both, square)

        carry = (both, square)
        forwards = []
        for dx in reversed(COLUMN_ORDER):
            b = lax.rem(cx + dx, SIDE)
            for dy in reversed(COLUMN_ORDER):
                if (dx, dy) != (0, 0):
                    source = chip_at(dx, dy)
                    a = lax.rem(cy + dy, SIDE)
                    remote(
                        x_v.at[core, b, a], x_v.at[core, b, a],
                        all_ssem.at[source], all_rsem.at[source], source * 2 + core,
                    ).wait_recv()
            copy = remote(
                x_v.at[core, b], x_v.at[core, b], fwd_ssem.at[b], fwd_rsem.at[b], partner
            )
            copy.start()
            sends.append(copy)
            carry = multiply(core, b, carry)
        for dx in reversed(COLUMN_ORDER):
            b = lax.rem(cx + dx, SIDE)
            remote(
                x_v.at[other, b], x_v.at[other, b], fwd_ssem.at[b], fwd_rsem.at[b], partner
            ).wait_recv()
            carry = multiply(other, b, carry)
        both, square = carry
        both = both * lax.rsqrt(square / width + 1e-6)
        gate = both[:, :hidden]
        up = both[:, hidden:]
        mlp_ref[...] = (gate / (1.0 + jnp.exp(-gate)) * up).astype(jnp.bfloat16)

        first = lax.rem(chip, SIDE) * (2 * req) + core * req
        line = lax.broadcasted_iota(jnp.int32, (rows, block), 0)
        for which in range(2):
            for b in range(SIDE):
                x = x_v[which, b, cy].astype(jnp.float32)
                picked = jnp.concatenate(
                    [
                        jnp.sum(jnp.where(line == first + r, x, 0.0), axis=0, keepdims=True)
                        for r in range(req)
                    ],
                    axis=0,
                )
                at = which * half + b * block
                att_ref[:, at : at + block] = picked.astype(jnp.bfloat16)

        for copy in sends + [trade_wuv] + trade_w2 + trade_hid:
            copy.wait_send()

    return kernel


def per_device(hidden_in, queries, cache, lengths, w_uv, w_out, norm_gain, w_gate, w_up):
    req, heads, depth = queries.shape
    positions = cache.shape[1]
    latent, value = w_uv.shape[1:]
    width, hidden = w_gate.shape
    rotary = depth - latent
    tokens = req * 2 * CHIPS
    half = width // 2
    block = half // SIDE
    rows = tokens // SIDE
    size = CHIPS * 16
    bf16 = jnp.bfloat16
    dma = pltpu.SemaphoreType.DMA
    hbm = pl.BlockSpec(memory_space=pltpu.HBM)
    vmem = pl.BlockSpec(memory_space=pltpu.VMEM)
    return pl.pallas_call(
        make_kernel(req, heads, latent, value, rotary, width, hidden, positions),
        out_shape=(
            jax.ShapeDtypeStruct((req, width), bf16),
            jax.ShapeDtypeStruct((tokens, hidden), bf16),
        ),
        in_specs=[hbm] * 9,
        out_specs=(vmem, vmem),
        scratch_shapes=[
            pltpu.SMEM((req,), jnp.int32),
            pltpu.VMEM((req, heads, depth), bf16),
            pltpu.VMEM((req, positions, depth), bf16),
            pltpu.VMEM((2, latent, value), bf16),
            pltpu.VMEM((SIDE, 2, value, block), bf16),
            pltpu.VMEM((SIDE, 2, req, block), bf16),
            pltpu.VMEM((width // LANES, LANES), bf16),
            pltpu.VMEM((2 * SIDE, 1, block), jnp.float32),
            pltpu.VMEM((2 * SIDE, 2 * hidden, block), bf16),
            pltpu.VMEM((size, size), bf16),
            pltpu.VMEM((size, size), bf16),
            pltpu.VMEM((CHIPS, 16, LANES), bf16),
            pltpu.VMEM((2 * CHIPS, 16, LANES), bf16),
            pltpu.VMEM((SIDE, SIDE, rows, block), bf16),
            pltpu.VMEM((CHIPS, rows, block), bf16),
            pltpu.VMEM((2, SIDE, SIDE, rows, block), bf16),
            dma((5,)),
            dma((SIDE,)),
            dma((SIDE,)),
            dma((4 * SIDE,)),
            dma((SIDE,)),
            dma((SIDE,)),
            dma((SIDE,)),
            dma((SIDE,)),
            dma((1,)),
            dma((1,)),
            dma((2 * CHIPS,)),
            dma((2 * CHIPS,)),
            dma((CHIPS,)),
            dma((CHIPS,)),
            dma((CHIPS,)),
            dma((CHIPS,)),
            dma((SIDE,)),
            dma((SIDE,)),
        ],
        compiler_params=pltpu.CompilerParams(
            collective_id=0, has_side_effects=True, vmem_limit_bytes=60 * 1024 * 1024
        ),
    )(
        lengths, hidden_in, queries, cache, w_uv, w_out,
        norm_gain.reshape(width // LANES, LANES), w_gate.T, w_up.T,
    )


def solution(mesh):
    in_specs = (
        P(("group", "tp"), None),
        P(("group", "tp"), None, None),
        P(("group", "tp"), None, None),
        P(("group", "tp")),
        P("tp", None, None),
        P("tp", None),
        P(),
        P(None, "tp"),
        P(None, "tp"),
    )
    out_specs = (P(("group", "tp"), None), P("group", "tp"))
    return jax.shard_map(
        per_device, mesh=mesh, in_specs=in_specs, out_specs=out_specs, check_vma=False
    )
```

```python
import math

import jax
import jax.numpy as jnp
from jax import lax
from jax.experimental import pallas as pl
from jax.experimental.pallas import tpu as pltpu
from jax.sharding import PartitionSpec as P

MESH = pl.DeviceIdType.MESH
SIDE = 4
CHIPS = SIDE * SIDE
LANES = 128
OFFSETS = sorted(
    ((dx, dy) for dx in range(SIDE) for dy in range(SIDE)),
    key=lambda o: -(min(o[0], SIDE - o[0]) + min(o[1], SIDE - o[1])),
)
COLUMN_ORDER = (2, 1, 3, 0)
PIECES = ((0, 256), (256, 512), (512, 896))


def make_kernel(req, heads, latent, value, rotary, width, hidden, positions):
    tokens = req * 2 * CHIPS
    half = width // 2
    block = half // SIDE
    rows = tokens // SIDE
    score_scale = 1.0 / math.sqrt(value + rotary)
    pieces = latent // LANES

    def kernel(
        lengths_hbm, hid_hbm, q_hbm, cache_hbm, wuv_hbm, wout_hbm, gain_hbm, wg_hbm, wu_hbm,
        att_ref, mlp_ref,
        lengths_s, q_v, cache_v, wuv_v, w2_v, hid_v, gain_v, gain_f, wg_v, wu_v, wg_t, wu_t, send_perm, recv_perm,
        ctx_send, ctx_recv, part_v, red_v, x_v,
        in_sem, w2_sem, hid_sem, mlp_sem, w2x_send, w2x_recv, hidx_send, hidx_recv, wuvx_send, wuvx_recv,
        ctx_ssem, ctx_rsem, red_ssem, red_rsem, all_ssem, all_rsem, fwd_ssem, fwd_rsem,
    ):
        group = lax.axis_index("group")
        me = lax.axis_index("tp")
        core = lax.rem(me, 2)
        other = 1 - core
        chip = me // 2
        cx = lax.rem(chip, SIDE)
        cy = chip // SIDE

        def chip_at(dx, dy):
            return lax.rem(cy + dy, SIDE) * SIDE + lax.rem(cx + dx, SIDE)

        def remote(src, dst, ssem, rsem, target):
            return pltpu.make_async_remote_copy(
                src_ref=src, dst_ref=dst, send_sem=ssem, recv_sem=rsem,
                device_id=(group, target), device_id_type=MESH,
            )

        partner = chip * 2 + other

        load_cache = pltpu.make_async_copy(cache_hbm, cache_v, in_sem.at[0])
        load_q = pltpu.make_async_copy(q_hbm, q_v, in_sem.at[1])
        load_lengths = pltpu.make_async_copy(lengths_hbm, lengths_s, in_sem.at[3])
        load_gain = pltpu.make_async_copy(gain_hbm, gain_v, in_sem.at[4])
        load_cache.start()
        load_q.start()
        load_lengths.start()
        load_gain.start()
        barrier = pltpu.get_barrier_semaphore()
        for dx, dy in OFFSETS:
            for dc in range(2):
                if (dx, dy, dc) != (0, 0, 0):
                    target = chip_at(dx, dy) * 2 + lax.rem(core + dc, 2)
                    pl.semaphore_signal(
                        barrier, inc=1, device_id=(group, target), device_id_type=MESH
                    )

        size = CHIPS * 16
        row = lax.broadcasted_iota(jnp.int32, (size, size), 0)
        col = lax.broadcasted_iota(jnp.int32, (size, size), 1)
        to = row // 16
        item = row % 16
        src_row = ((item % 2) * pieces + (item // 2) % pieces) * heads + to * 2 + item // (2 * pieces)
        send_perm[...] = (col == src_row).astype(jnp.bfloat16)
        tok = row % 32
        src_row = (tok // 2) * 16 + (row // 32) * 2 + tok % 2
        recv_perm[...] = (col == src_row).astype(jnp.bfloat16)

        load_lengths.wait()
        load_cache.wait()
        load_q.wait()

        load_wuv = pltpu.make_async_copy(wuv_hbm.at[0], wuv_v.at[core], in_sem.at[2])
        load_wuv.start()

        def columns(which, b):
            return pl.ds(pl.multiple_of(which * half + b * block, LANES), block)

        loads_w2 = []
        loads_hid = []
        for b in range(SIDE):
            loads_w2.append(
                pltpu.make_async_copy(
                    wout_hbm.at[:, columns(core, b)], w2_v.at[b, core], w2_sem.at[b]
                )
            )
            loads_hid.append(
                pltpu.make_async_copy(
                    hid_hbm.at[:, columns(core, b)], hid_v.at[b, core], hid_sem.at[b]
                )
            )
        for copy in loads_w2 + loads_hid:
            copy.start()
        loads_mlp = []
        for k in range(2 * SIDE):
            for i, (src, dst) in enumerate(((wg_hbm, wg_v), (wu_hbm, wu_v))):
                loads_mlp.append(
                    pltpu.make_async_copy(
                        src.at[:, pl.ds(k * block, block)], dst.at[k], mlp_sem.at[2 * k + i]
                    )
                )
        for copy in loads_mlp:
            copy.start()

        position = lax.broadcasted_iota(jnp.int32, (heads, positions), 1)
        parts = []
        for r in range(req):
            keys = cache_v[r]
            scores = (
                lax.dot_general(
                    q_v[r], keys, (((1,), (1,)), ((), ())), preferred_element_type=jnp.float32
                )
                * score_scale
            )
            visible = position < lengths_s[r]
            top = jnp.max(jnp.where(visible, scores, -1e30), axis=-1, keepdims=True)
            probs = jnp.exp(jnp.where(visible, scores - top, -1e30))
            total = jnp.sum(probs, axis=-1, keepdims=True)
            summed = jnp.dot(
                probs.astype(jnp.bfloat16), keys[:, :latent], preferred_element_type=jnp.float32
            )
            ctx = (summed / total).astype(jnp.bfloat16)
            for p in range(pieces):
                parts.append(ctx[:, p * LANES : (p + 1) * LANES])
        ctx_send[...] = (
            jnp.dot(
                send_perm[...], jnp.concatenate(parts, axis=0), preferred_element_type=jnp.float32
            )
            .astype(jnp.bfloat16)
            .reshape(CHIPS, 16, LANES)
        )

        load_gain.wait()
        gains = gain_v[...].astype(jnp.float32)
        for k in range(2 * SIDE):
            for i in range(block // LANES):
                at = k * (block // LANES) + i
                gain_f[k, 0:1, i * LANES : (i + 1) * LANES] = gains[at : at + 1, :]

        pl.semaphore_wait(barrier, 2 * CHIPS - 1)

        sends = []
        for dx, dy in OFFSETS:
            for dc in range(2):
                if (dx, dy, dc) != (0, 0, 0):
                    to_chip = chip_at(dx, dy)
                    target = to_chip * 2 + lax.rem(core + dc, 2)
                    copy = remote(
                        ctx_send.at[to_chip], ctx_recv.at[me],
                        ctx_ssem.at[target], ctx_rsem.at[me], target,
                    )
                    copy.start()
                    sends.append(copy)
        trade_wuv = remote(
            wuv_hbm.at[0], wuv_v.at[core], wuvx_send.at[0], wuvx_recv.at[0], partner
        )
        trade_wuv.start()
        trade_w2 = []
        trade_hid = []
        for b in range(SIDE):
            trade_w2.append(
                remote(
                    wout_hbm.at[:, columns(other, b)], w2_v.at[b, core],
                    w2x_send.at[b], w2x_recv.at[b], partner,
                )
            )
            trade_hid.append(
                remote(
                    hid_hbm.at[:, columns(other, b)], hid_v.at[b, core],
                    hidx_send.at[b], hidx_recv.at[b], partner,
                )
            )
        for copy in trade_w2 + trade_hid:
            copy.start()
        ctx_recv[me] = ctx_send[chip]

        for copy in [load_wuv] + loads_w2 + loads_hid:
            copy.wait()
        trade_wuv.wait_recv()
        for copy in trade_w2 + trade_hid:
            copy.wait_recv()
        for dx, dy in reversed(OFFSETS):
            for dc in range(2):
                if (dx, dy, dc) != (0, 0, 0):
                    source = chip_at(dx, dy) * 2 + lax.rem(core + dc, 2)
                    remote(
                        ctx_send.at[0], ctx_recv.at[source],
                        ctx_ssem.at[source], ctx_rsem.at[source], source,
                    ).wait_recv()

        got = ctx_recv[...].reshape(2, size, LANES)
        ordered = [
            jnp.dot(recv_perm[...], got[k], preferred_element_type=jnp.float32).astype(jnp.bfloat16)
            for k in range(2)
        ]
        vals = []
        for h in range(2):
            ctx = jnp.concatenate(
                [
                    jnp.concatenate(
                        [o[(h * pieces + p) * 32 : (h * pieces + p + 1) * 32] for p in range(pieces)],
                        axis=1,
                    )
                    for o in ordered
                ],
                axis=0,
            )
            vals.append(
                jnp.dot(ctx, wuv_v[h], preferred_element_type=jnp.float32).astype(jnp.bfloat16)
            )
        vals = jnp.concatenate(vals, axis=1)

        token = lax.broadcasted_iota(jnp.int32, (tokens, block), 0)

        def reduce_copy(piece, dx, dy):
            low, high = PIECES[piece]
            to_chip = chip_at(dx, dy)
            return remote(
                part_v.at[lax.rem(cx + dx, SIDE), lax.rem(cy + dy, SIDE), :, low:high],
                red_v.at[chip, :, low:high],
                red_ssem.at[piece * CHIPS + to_chip], red_rsem.at[piece * CHIPS + chip],
                to_chip * 2 + core,
            )

        for dx in COLUMN_ORDER:
            b = lax.rem(cx + dx, SIDE)
            part = jnp.dot(
                vals, w2_v[b].reshape(2 * value, block), preferred_element_type=jnp.float32
            )
            own = hid_v[b].astype(jnp.float32)
            for h in range(2):
                for r in range(req):
                    part = part + jnp.where(
                        token == chip * (2 * req) + h * req + r, own[h, r : r + 1, :], 0.0
                    )
            part_v[b] = part.astype(jnp.bfloat16).reshape(SIDE, rows, block)
            for dy in COLUMN_ORDER:
                if (dx, dy) != (0, 0):
                    copy = reduce_copy(0, dx, dy)
                    copy.start()
                    sends.append(copy)
        for piece in range(1, len(PIECES)):
            for dx in COLUMN_ORDER:
                for dy in COLUMN_ORDER:
                    if (dx, dy) != (0, 0):
                        copy = reduce_copy(piece, dx, dy)
                        copy.start()
                        sends.append(copy)
        red_v[chip] = part_v[cx, cy]

        for copy in loads_mlp:
            copy.wait()

        def turn(k, carry):
            wg_t[k] = wg_v[k].T
            wu_t[k] = wu_v[k].T
            return carry

        lax.fori_loop(0, 2 * SIDE, turn, 0)

        for piece, (low, high) in enumerate(PIECES):
            for dx, dy in reversed(OFFSETS):
                if (dx, dy) != (0, 0):
                    source = chip_at(dx, dy)
                    at = piece * CHIPS + source
                    remote(
                        part_v.at[0, 0, :, low:high], red_v.at[source, :, low:high],
                        red_ssem.at[at], red_rsem.at[at], source * 2 + core,
                    ).wait_recv()
            total = red_v[0, :, low:high].astype(jnp.float32)
            for k in range(1, CHIPS):
                total = total + red_v[k, :, low:high].astype(jnp.float32)
            x_v[core, cx, cy, :, low:high] = total.astype(jnp.bfloat16)
            for dx, dy in OFFSETS:
                if (dx, dy) != (0, 0):
                    to_chip = chip_at(dx, dy)
                    spot = x_v.at[core, cx, cy, :, low:high]
                    copy = remote(
                        spot, spot, all_ssem.at[piece * CHIPS + to_chip],
                        all_rsem.at[piece * CHIPS + chip], to_chip * 2 + core,
                    )
                    copy.start()
                    sends.append(copy)

        def multiply(which, b, low, high, carry):
            gate, up, square = carry
            k = which * SIDE + b
            x = x_v[which, b, :, :, low:high].reshape(tokens, high - low).astype(jnp.float32)
            square = square + jnp.sum(x * x, axis=-1, keepdims=True)
            x = (x * gain_f[k, :, low:high]).astype(jnp.bfloat16)
            gate = gate + jnp.dot(x, wg_t[k, low:high, :], preferred_element_type=jnp.float32)
            up = up + jnp.dot(x, wu_t[k, low:high, :], preferred_element_type=jnp.float32)
            return (gate, up, square)

        carry = (
            jnp.zeros((tokens, hidden), jnp.float32),
            jnp.zeros((tokens, hidden), jnp.float32),
            jnp.zeros((tokens, 1), jnp.float32),
        )
        for piece, (low, high) in enumerate(PIECES):
            for dx in reversed(COLUMN_ORDER):
                b = lax.rem(cx + dx, SIDE)
                for dy in reversed(COLUMN_ORDER):
                    if (dx, dy) != (0, 0):
                        source = chip_at(dx, dy)
                        at = piece * CHIPS + source
                        spot = x_v.at[core, b, lax.rem(cy + dy, SIDE), :, low:high]
                        remote(
                            spot, spot, all_ssem.at[at], all_rsem.at[at], source * 2 + core
                        ).wait_recv()
                spot = x_v.at[core, b, :, :, low:high]
                at = piece * SIDE + b
                copy = remote(spot, spot, fwd_ssem.at[at], fwd_rsem.at[at], partner)
                copy.start()
                sends.append(copy)
                carry = multiply(core, b, low, high, carry)
            for dx in reversed(COLUMN_ORDER):
                b = lax.rem(cx + dx, SIDE)
                spot = x_v.at[other, b, :, :, low:high]
                at = piece * SIDE + b
                remote(spot, spot, fwd_ssem.at[at], fwd_rsem.at[at], partner).wait_recv()
                carry = multiply(other, b, low, high, carry)
        gate, up, square = carry
        scale = lax.rsqrt(square / width + 1e-6)
        gate = gate * scale
        up = up * scale
        mlp_ref[...] = (gate / (1.0 + jnp.exp(-gate)) * up).astype(jnp.bfloat16)

        first = lax.rem(chip, SIDE) * (2 * req) + core * req
        line = lax.broadcasted_iota(jnp.int32, (rows, block), 0)
        for which in range(2):
            for b in range(SIDE):
                x = x_v[which, b, cy].astype(jnp.float32)
                picked = jnp.concatenate(
                    [
                        jnp.sum(jnp.where(line == first + r, x, 0.0), axis=0, keepdims=True)
                        for r in range(req)
                    ],
                    axis=0,
                )
                at = which * half + b * block
                att_ref[:, at : at + block] = picked.astype(jnp.bfloat16)

        for copy in sends + [trade_wuv] + trade_w2 + trade_hid:
            copy.wait_send()

    return kernel


def write_out(att_ref, mlp_ref, att_hbm, mlp_hbm, sem):
    copies = (
        pltpu.make_async_copy(att_ref, att_hbm, sem.at[0]),
        pltpu.make_async_copy(mlp_ref, mlp_hbm, sem.at[1]),
    )
    for copy in copies:
        copy.start()
    for copy in copies:
        copy.wait()


def per_device(hidden_in, queries, cache, lengths, w_uv, w_out, norm_gain, w_gate, w_up):
    req, heads, depth = queries.shape
    positions = cache.shape[1]
    latent, value = w_uv.shape[1:]
    width, hidden = w_gate.shape
    rotary = depth - latent
    tokens = req * 2 * CHIPS
    half = width // 2
    block = half // SIDE
    rows = tokens // SIDE
    size = CHIPS * 16
    bf16 = jnp.bfloat16
    dma = pltpu.SemaphoreType.DMA
    hbm = pl.BlockSpec(memory_space=pltpu.HBM)
    vmem = pl.BlockSpec(memory_space=pltpu.VMEM)
    outs = (
        jax.ShapeDtypeStruct((req, width), bf16),
        jax.ShapeDtypeStruct((tokens, hidden), bf16),
    )
    att, mlp = pl.pallas_call(
        make_kernel(req, heads, latent, value, rotary, width, hidden, positions),
        out_shape=outs,
        in_specs=[hbm] * 9,
        out_specs=(vmem, vmem),
        scratch_shapes=[
            pltpu.SMEM((req,), jnp.int32),
            pltpu.VMEM((req, heads, depth), bf16),
            pltpu.VMEM((req, positions, depth), bf16),
            pltpu.VMEM((2, latent, value), bf16),
            pltpu.VMEM((SIDE, 2, value, block), bf16),
            pltpu.VMEM((SIDE, 2, req, block), bf16),
            pltpu.VMEM((width // LANES, LANES), bf16),
            pltpu.VMEM((2 * SIDE, 1, block), jnp.float32),
            pltpu.VMEM((2 * SIDE, hidden, block), bf16),
            pltpu.VMEM((2 * SIDE, hidden, block), bf16),
            pltpu.VMEM((2 * SIDE, block, hidden), bf16),
            pltpu.VMEM((2 * SIDE, block, hidden), bf16),
            pltpu.VMEM((size, size), bf16),
            pltpu.VMEM((size, size), bf16),
            pltpu.VMEM((CHIPS, 16, LANES), bf16),
            pltpu.VMEM((2 * CHIPS, 16, LANES), bf16),
            pltpu.VMEM((SIDE, SIDE, rows, block), bf16),
            pltpu.VMEM((CHIPS, rows, block), bf16),
            pltpu.VMEM((2, SIDE, SIDE, rows, block), bf16),
            dma((5,)),
            dma((SIDE,)),
            dma((SIDE,)),
            dma((4 * SIDE,)),
            dma((SIDE,)),
            dma((SIDE,)),
            dma((SIDE,)),
            dma((SIDE,)),
            dma((1,)),
            dma((1,)),
            dma((2 * CHIPS,)),
            dma((2 * CHIPS,)),
            dma((len(PIECES) * CHIPS,)),
            dma((len(PIECES) * CHIPS,)),
            dma((len(PIECES) * CHIPS,)),
            dma((len(PIECES) * CHIPS,)),
            dma((len(PIECES) * SIDE,)),
            dma((len(PIECES) * SIDE,)),
        ],
        compiler_params=pltpu.CompilerParams(
            collective_id=0, has_side_effects=True, vmem_limit_bytes=40 * 1024 * 1024
        ),
    )(
        *(
            pltpu.with_memory_space_constraint(operand, pltpu.HBM)
            for operand in (
                lengths, hidden_in, queries, cache, w_uv, w_out,
                norm_gain.reshape(width // LANES, LANES), w_gate.T, w_up.T,
            )
        )
    )
    return pl.pallas_call(
        write_out,
        out_shape=outs,
        in_specs=[vmem, vmem],
        out_specs=(hbm, hbm),
        scratch_shapes=[dma((2,))],
        compiler_params=pltpu.CompilerParams(vmem_limit_bytes=1024 * 1024),
    )(att, mlp)


def solution(mesh):
    in_specs = (
        P(("group", "tp"), None),
        P(("group", "tp"), None, None),
        P(("group", "tp"), None, None),
        P(("group", "tp")),
        P("tp", None, None),
        P("tp", None),
        P(),
        P(None, "tp"),
        P(None, "tp"),
    )
    out_specs = (P(("group", "tp"), None), P("group", "tp"))
    return jax.shard_map(
        per_device, mesh=mesh, in_specs=in_specs, out_specs=out_specs, check_vma=False
    )
```

```python
import math

import jax
import jax.numpy as jnp
from jax import lax
from jax.experimental import pallas as pl
from jax.experimental.pallas import tpu as pltpu
from jax.sharding import PartitionSpec as P

MESH = pl.DeviceIdType.MESH
SIDE = 4
CHIPS = SIDE * SIDE
LANES = 128
OFFSETS = sorted(
    ((dx, dy) for dx in range(SIDE) for dy in range(SIDE)),
    key=lambda o: -(min(o[0], SIDE - o[0]) + min(o[1], SIDE - o[1])),
)
COLUMN_ORDER = (2, 1, 3, 0)
PIECES = ((0, 256), (256, 512), (512, 896))


def make_kernel(req, heads, latent, value, rotary, width, hidden, positions):
    tokens = req * 2 * CHIPS
    half = width // 2
    block = half // SIDE
    rows = tokens // SIDE
    score_scale = 1.0 / math.sqrt(value + rotary)
    pieces = latent // LANES

    def kernel(
        lengths_hbm, hid_hbm, q_hbm, cache_hbm, wuv_hbm, wout_hbm, gain_hbm, wg_hbm, wu_hbm,
        att_ref, mlp_ref,
        lengths_s, q_v, cache_v, wuv_v, w2_v, hid_v, gain_v, gain_f, wg_v, wu_v, wg_t, wu_t, send_perm, recv_perm,
        ctx_send, ctx_recv, part_v, red_v, x_v,
        in_sem, w2_sem, hid_sem, mlp_sem, w2x_send, w2x_recv, hidx_send, hidx_recv, wuvx_send, wuvx_recv,
        ctx_ssem, ctx_rsem, red_ssem, red_rsem, all_ssem, all_rsem, fwd_ssem, fwd_rsem,
    ):
        group = lax.axis_index("group")
        me = lax.axis_index("tp")
        core = lax.rem(me, 2)
        other = 1 - core
        chip = me // 2
        cx = lax.rem(chip, SIDE)
        cy = chip // SIDE

        def chip_at(dx, dy):
            return lax.rem(cy + dy, SIDE) * SIDE + lax.rem(cx + dx, SIDE)

        def remote(src, dst, ssem, rsem, target):
            return pltpu.make_async_remote_copy(
                src_ref=src, dst_ref=dst, send_sem=ssem, recv_sem=rsem,
                device_id=(group, target), device_id_type=MESH,
            )

        partner = chip * 2 + other

        load_cache = pltpu.make_async_copy(cache_hbm, cache_v, in_sem.at[0])
        load_q = pltpu.make_async_copy(q_hbm, q_v, in_sem.at[1])
        load_lengths = pltpu.make_async_copy(lengths_hbm, lengths_s, in_sem.at[3])
        load_gain = pltpu.make_async_copy(gain_hbm, gain_v, in_sem.at[4])
        load_cache.start()
        load_q.start()
        load_lengths.start()
        load_gain.start()
        barrier = pltpu.get_barrier_semaphore()
        for dx, dy in OFFSETS:
            for dc in range(2):
                if (dx, dy, dc) != (0, 0, 0):
                    target = chip_at(dx, dy) * 2 + lax.rem(core + dc, 2)
                    pl.semaphore_signal(
                        barrier, inc=1, device_id=(group, target), device_id_type=MESH
                    )

        size = CHIPS * 16
        row = lax.broadcasted_iota(jnp.int32, (size, size), 0)
        col = lax.broadcasted_iota(jnp.int32, (size, size), 1)
        to = row // 16
        item = row % 16
        src_row = ((item % 2) * pieces + (item // 2) % pieces) * heads + to * 2 + item // (2 * pieces)
        send_perm[...] = (col == src_row).astype(jnp.bfloat16)
        tok = row % 32
        src_row = (tok // 2) * 16 + (row // 32) * 2 + tok % 2
        recv_perm[...] = (col == src_row).astype(jnp.bfloat16)

        load_lengths.wait()
        load_cache.wait()
        load_q.wait()

        position = lax.broadcasted_iota(jnp.int32, (heads, positions), 1)
        parts = []
        for r in range(req):
            keys = cache_v[r]
            scores = (
                lax.dot_general(
                    q_v[r], keys, (((1,), (1,)), ((), ())), preferred_element_type=jnp.float32
                )
                * score_scale
            )
            visible = position < lengths_s[r]
            top = jnp.max(jnp.where(visible, scores, -1e30), axis=-1, keepdims=True)
            probs = jnp.exp(jnp.where(visible, scores - top, -1e30))
            total = jnp.sum(probs, axis=-1, keepdims=True)
            summed = jnp.dot(
                probs.astype(jnp.bfloat16), keys[:, :latent], preferred_element_type=jnp.float32
            )
            ctx = (summed / total).astype(jnp.bfloat16)
            for p in range(pieces):
                parts.append(ctx[:, p * LANES : (p + 1) * LANES])
        ctx_send[...] = (
            jnp.dot(
                send_perm[...], jnp.concatenate(parts, axis=0), preferred_element_type=jnp.float32
            )
            .astype(jnp.bfloat16)
            .reshape(CHIPS, 16, LANES)
        )

        load_gain.wait()
        gains = gain_v[...].astype(jnp.float32)
        for k in range(2 * SIDE):
            for i in range(block // LANES):
                at = k * (block // LANES) + i
                gain_f[k, 0:1, i * LANES : (i + 1) * LANES] = gains[at : at + 1, :]

        pl.semaphore_wait(barrier, 2 * CHIPS - 1)

        for dx, dy in OFFSETS:
            for dc in range(2):
                if (dx, dy, dc) != (0, 0, 0):
                    to_chip = chip_at(dx, dy)
                    target = to_chip * 2 + lax.rem(core + dc, 2)
                    copy = remote(
                        ctx_send.at[to_chip], ctx_recv.at[me],
                        ctx_ssem.at[0], ctx_rsem.at[0], target,
                    )
                    copy.start()
        def half_of(which):
            return pl.ds(pl.multiple_of(which * half, LANES), half)

        load_w2 = pltpu.make_async_copy(wout_hbm.at[:, half_of(core)], w2_v.at[core], w2_sem.at[0])
        trade_w2 = remote(
            wout_hbm.at[:, half_of(other)], w2_v.at[core], w2x_send.at[0], w2x_recv.at[0], partner
        )
        load_wuv = pltpu.make_async_copy(wuv_hbm.at[0], wuv_v.at[core], in_sem.at[2])
        trade_wuv = remote(
            wuv_hbm.at[0], wuv_v.at[core], wuvx_send.at[0], wuvx_recv.at[0], partner
        )
        load_hid = pltpu.make_async_copy(
            hid_hbm.at[:, half_of(core)], hid_v.at[core], hid_sem.at[0]
        )
        trade_hid = remote(
            hid_hbm.at[:, half_of(other)], hid_v.at[core], hidx_send.at[0], hidx_recv.at[0], partner
        )
        loads = (load_wuv, load_w2, load_hid)
        trades = (trade_wuv, trade_w2, trade_hid)
        for copy in trades + loads:
            copy.start()
        loads_mlp = []
        for k in range(2 * SIDE):
            for i, (src, dst) in enumerate(((wg_hbm, wg_v), (wu_hbm, wu_v))):
                loads_mlp.append(
                    pltpu.make_async_copy(
                        src.at[:, pl.ds(k * block, block)], dst.at[k], mlp_sem.at[2 * k + i]
                    )
                )
        for copy in loads_mlp:
            copy.start()
        ctx_recv[me] = ctx_send[chip]

        for copy in loads:
            copy.wait()
        for copy in trades:
            copy.wait_recv()
        others = ctx_recv.at[pl.ds(0, 2 * CHIPS - 1)]
        all_ctx = remote(others, others, ctx_ssem.at[0], ctx_rsem.at[0], partner)
        all_ctx.wait_recv()

        got = ctx_recv[...].reshape(2, size, LANES)
        ordered = [
            jnp.dot(recv_perm[...], got[k], preferred_element_type=jnp.float32).astype(jnp.bfloat16)
            for k in range(2)
        ]
        vals = []
        for h in range(2):
            ctx = jnp.concatenate(
                [
                    jnp.concatenate(
                        [o[(h * pieces + p) * 32 : (h * pieces + p + 1) * 32] for p in range(pieces)],
                        axis=1,
                    )
                    for o in ordered
                ],
                axis=0,
            )
            vals.append(
                jnp.dot(ctx, wuv_v[h], preferred_element_type=jnp.float32).astype(jnp.bfloat16)
            )
        vals = jnp.concatenate(vals, axis=1)

        token = lax.broadcasted_iota(jnp.int32, (tokens, block), 0)

        def reduce_copy(piece, dx, dy):
            to_chip = chip_at(dx, dy)
            return remote(
                part_v[piece].at[lax.rem(cx + dx, SIDE), lax.rem(cy + dy, SIDE)],
                red_v[piece].at[chip],
                red_ssem.at[piece], red_rsem.at[piece],
                to_chip * 2 + core,
            )

        def fifteen(piece, ssem, rsem):
            others = red_v[piece].at[pl.ds(0, CHIPS - 1)]
            return remote(others, others, ssem.at[piece], rsem.at[piece], partner)

        for dx in COLUMN_ORDER:
            b = lax.rem(cx + dx, SIDE)
            span = pl.ds(pl.multiple_of(b * block, LANES), block)
            part = jnp.dot(
                vals, w2_v[:, :, span].reshape(2 * value, block), preferred_element_type=jnp.float32
            )
            own = hid_v[:, :, span].astype(jnp.float32)
            for h in range(2):
                for r in range(req):
                    part = part + jnp.where(
                        token == chip * (2 * req) + h * req + r, own[h, r : r + 1, :], 0.0
                    )
            for piece, (low, high) in enumerate(PIECES):
                part_v[piece][b] = (
                    part[:, low:high].astype(jnp.bfloat16).reshape(SIDE, rows, high - low)
                )
            for dy in COLUMN_ORDER:
                if (dx, dy) != (0, 0):
                    reduce_copy(0, dx, dy).start()
        for piece in range(1, len(PIECES)):
            for dx in COLUMN_ORDER:
                for dy in COLUMN_ORDER:
                    if (dx, dy) != (0, 0):
                        reduce_copy(piece, dx, dy).start()
        for part, red in zip(part_v, red_v):
            red[chip] = part[cx, cy]

        for copy in loads_mlp:
            copy.wait()

        def turn(k, carry):
            wg_t[k] = wg_v[k].T
            wu_t[k] = wu_v[k].T
            return carry

        lax.fori_loop(0, 2 * SIDE, turn, 0)
        all_ctx.wait_send()
        for copy in trades:
            copy.wait_send()

        for piece in range(len(PIECES)):
            fifteen(piece, red_ssem, red_rsem).wait_recv()
            total = red_v[piece][0].astype(jnp.float32)
            for k in range(1, CHIPS):
                total = total + red_v[piece][k].astype(jnp.float32)
            x_v[piece][core, cx, cy] = total.astype(jnp.bfloat16)
            for dx, dy in OFFSETS:
                if (dx, dy) != (0, 0):
                    to_chip = chip_at(dx, dy)
                    spot = x_v[piece].at[core, cx, cy]
                    copy = remote(
                        spot, spot, all_ssem.at[piece],
                        all_rsem.at[piece], to_chip * 2 + core,
                    )
                    copy.start()

        def multiply(which, b, piece, carry):
            low, high = PIECES[piece]
            gate, up, square = carry
            k = which * SIDE + b
            x = x_v[piece][which, b].reshape(tokens, high - low).astype(jnp.float32)
            square = square + jnp.sum(x * x, axis=-1, keepdims=True)
            x = (x * gain_f[k, :, low:high]).astype(jnp.bfloat16)
            gate = gate + jnp.dot(x, wg_t[k, low:high, :], preferred_element_type=jnp.float32)
            up = up + jnp.dot(x, wu_t[k, low:high, :], preferred_element_type=jnp.float32)
            return (gate, up, square)

        carry = (
            jnp.zeros((tokens, hidden), jnp.float32),
            jnp.zeros((tokens, hidden), jnp.float32),
            jnp.zeros((tokens, 1), jnp.float32),
        )
        def forward(piece, which):
            spot = x_v[piece].at[which]
            return remote(spot, spot, fwd_ssem.at[piece], fwd_rsem.at[piece], partner)

        def own_blocks(piece, carry):
            fifteen(piece, all_ssem, all_rsem).wait_recv()
            forward(piece, core).start()
            for b in range(SIDE):
                carry = multiply(core, b, piece, carry)
            return carry

        def partner_blocks(piece, carry):
            forward(piece, other).wait_recv()
            for b in range(SIDE):
                carry = multiply(other, b, piece, carry)
            return carry

        first = lax.rem(chip, SIDE) * (2 * req) + core * req

        def keep_rows(which, piece):
            low, high = PIECES[piece]
            line = lax.broadcasted_iota(jnp.int32, (rows, high - low), 0)
            for b in range(SIDE):
                x = x_v[piece][which, b, cy].astype(jnp.float32)
                picked = [
                    jnp.sum(jnp.where(line == first + r, x, 0.0), axis=0, keepdims=True)
                    for r in range(req)
                ]
                at = pl.multiple_of(which * half + b * block + low, LANES)
                att_ref[:, pl.ds(at, high - low)] = jnp.concatenate(picked, axis=0).astype(
                    jnp.bfloat16
                )

        for piece in range(len(PIECES)):
            fifteen(piece, red_ssem, red_rsem).wait_send()
        last = len(PIECES) - 1
        for piece in range(last + 1):
            carry = own_blocks(piece, carry)
            if piece > 0:
                carry = partner_blocks(piece - 1, carry)
                keep_rows(other, piece - 1)
            keep_rows(core, piece)
        carry = partner_blocks(last, carry)
        gate, up, square = carry
        scale = lax.rsqrt(square / width + 1e-6)
        gate = gate * scale
        up = up * scale
        mlp_ref[...] = (gate / (1.0 + jnp.exp(-gate)) * up).astype(jnp.bfloat16)

        keep_rows(other, last)

        for piece in range(len(PIECES)):
            fifteen(piece, all_ssem, red_rsem).wait_send()
        for piece in range(len(PIECES)):
            forward(piece, core).wait_send()

    return kernel


def write_out(att_ref, mlp_ref, att_hbm, mlp_hbm, sem):
    copies = (
        pltpu.make_async_copy(att_ref, att_hbm, sem.at[0]),
        pltpu.make_async_copy(mlp_ref, mlp_hbm, sem.at[1]),
    )
    for copy in copies:
        copy.start()
    for copy in copies:
        copy.wait()


def per_device(hidden_in, queries, cache, lengths, w_uv, w_out, norm_gain, w_gate, w_up):
    req, heads, depth = queries.shape
    positions = cache.shape[1]
    latent, value = w_uv.shape[1:]
    width, hidden = w_gate.shape
    rotary = depth - latent
    tokens = req * 2 * CHIPS
    half = width // 2
    block = half // SIDE
    rows = tokens // SIDE
    size = CHIPS * 16
    bf16 = jnp.bfloat16
    dma = pltpu.SemaphoreType.DMA
    hbm = pl.BlockSpec(memory_space=pltpu.HBM)
    vmem = pl.BlockSpec(memory_space=pltpu.VMEM)
    outs = (
        jax.ShapeDtypeStruct((req, width), bf16),
        jax.ShapeDtypeStruct((tokens, hidden), bf16),
    )
    att, mlp = pl.pallas_call(
        make_kernel(req, heads, latent, value, rotary, width, hidden, positions),
        out_shape=outs,
        in_specs=[hbm] * 9,
        out_specs=(vmem, vmem),
        scratch_shapes=[
            pltpu.SMEM((req,), jnp.int32),
            pltpu.VMEM((req, heads, depth), bf16),
            pltpu.VMEM((req, positions, depth), bf16),
            pltpu.VMEM((2, latent, value), bf16),
            pltpu.VMEM((2, value, half), bf16),
            pltpu.VMEM((2, req, half), bf16),
            pltpu.VMEM((width // LANES, LANES), bf16),
            pltpu.VMEM((2 * SIDE, 1, block), jnp.float32),
            pltpu.VMEM((2 * SIDE, hidden, block), bf16),
            pltpu.VMEM((2 * SIDE, hidden, block), bf16),
            pltpu.VMEM((2 * SIDE, block, hidden), bf16),
            pltpu.VMEM((2 * SIDE, block, hidden), bf16),
            pltpu.VMEM((size, size), bf16),
            pltpu.VMEM((size, size), bf16),
            pltpu.VMEM((CHIPS, 16, LANES), bf16),
            pltpu.VMEM((2 * CHIPS, 16, LANES), bf16),
            [pltpu.VMEM((SIDE, SIDE, rows, high - low), bf16) for low, high in PIECES],
            [pltpu.VMEM((CHIPS, rows, high - low), bf16) for low, high in PIECES],
            [pltpu.VMEM((2, SIDE, SIDE, rows, high - low), bf16) for low, high in PIECES],
            dma((5,)),
            dma((1,)),
            dma((1,)),
            dma((4 * SIDE,)),
            dma((1,)),
            dma((1,)),
            dma((1,)),
            dma((1,)),
            dma((1,)),
            dma((1,)),
            dma((1,)),
            dma((1,)),
            dma((len(PIECES),)),
            dma((len(PIECES),)),
            dma((len(PIECES),)),
            dma((len(PIECES),)),
            dma((len(PIECES),)),
            dma((len(PIECES),)),
        ],
        compiler_params=pltpu.CompilerParams(
            collective_id=0, has_side_effects=True, vmem_limit_bytes=40 * 1024 * 1024
        ),
    )(
        *(
            pltpu.with_memory_space_constraint(operand, pltpu.HBM)
            for operand in (
                lengths, hidden_in, queries, cache, w_uv, w_out,
                norm_gain.reshape(width // LANES, LANES), w_gate.T, w_up.T,
            )
        )
    )
    return pl.pallas_call(
        write_out,
        out_shape=outs,
        in_specs=[vmem, vmem],
        out_specs=(hbm, hbm),
        scratch_shapes=[dma((2,))],
        compiler_params=pltpu.CompilerParams(vmem_limit_bytes=1024 * 1024),
    )(att, mlp)


def solution(mesh):
    in_specs = (
        P(("group", "tp"), None),
        P(("group", "tp"), None, None),
        P(("group", "tp"), None, None),
        P(("group", "tp")),
        P("tp", None, None),
        P("tp", None),
        P(),
        P(None, "tp"),
        P(None, "tp"),
    )
    out_specs = (P(("group", "tp"), None), P("group", "tp"))
    return jax.shard_map(
        per_device, mesh=mesh, in_specs=in_specs, out_specs=out_specs, check_vma=False
    )
```

```python
import math

import jax
import jax.numpy as jnp
from jax import lax
from jax.experimental import pallas as pl
from jax.experimental.pallas import tpu as pltpu
from jax.sharding import PartitionSpec as P

MESH = pl.DeviceIdType.MESH
SIDE = 4
CHIPS = SIDE * SIDE
LANES = 128
OFFSETS = sorted(
    ((dx, dy) for dx in range(SIDE) for dy in range(SIDE)),
    key=lambda o: -(min(o[0], SIDE - o[0]) + min(o[1], SIDE - o[1])),
)
COLUMN_ORDER = (2, 1, 3, 0)
PIECES = ((0, 256), (256, 512), (512, 768), (768, 896))


def make_kernel(req, heads, latent, value, rotary, width, hidden, positions):
    tokens = req * 2 * CHIPS
    half = width // 2
    block = half // SIDE
    rows = tokens // SIDE
    score_scale = 1.0 / math.sqrt(value + rotary)
    pieces = latent // LANES

    def kernel(
        lengths_hbm, hid_hbm, q_hbm, cache_hbm, wuv_hbm, wout_hbm, gain_hbm, wg_hbm, wu_hbm,
        att_ref, mlp_ref,
        lengths_s, q_v, cache_v, wuv_v, w2_v, hid_v, gain_v, gain_f, wg_v, wu_v, wg_t, wu_t, send_perm, recv_perm,
        ctx_send, ctx_recv, part_v, red_v, x_v,
        in_sem, w2_sem, hid_sem, mlp_sem, w2x_send, w2x_recv, hidx_send, hidx_recv, wuvx_send, wuvx_recv,
        ctx_ssem, ctx_rsem, red_ssem, red_rsem, all_ssem, all_rsem, fwd_ssem, fwd_rsem,
    ):
        group = lax.axis_index("group")
        me = lax.axis_index("tp")
        core = lax.rem(me, 2)
        other = 1 - core
        chip = me // 2
        cx = lax.rem(chip, SIDE)
        cy = chip // SIDE

        def chip_at(dx, dy):
            return lax.rem(cy + dy, SIDE) * SIDE + lax.rem(cx + dx, SIDE)

        def remote(src, dst, ssem, rsem, target):
            return pltpu.make_async_remote_copy(
                src_ref=src, dst_ref=dst, send_sem=ssem, recv_sem=rsem,
                device_id=(group, target), device_id_type=MESH,
            )

        partner = chip * 2 + other

        load_cache = pltpu.make_async_copy(cache_hbm, cache_v, in_sem.at[0])
        load_q = pltpu.make_async_copy(q_hbm, q_v, in_sem.at[1])
        load_lengths = pltpu.make_async_copy(lengths_hbm, lengths_s, in_sem.at[3])
        load_gain = pltpu.make_async_copy(gain_hbm, gain_v, in_sem.at[4])
        load_cache.start()
        load_q.start()
        load_lengths.start()
        load_gain.start()
        barrier = pltpu.get_barrier_semaphore()
        for dx, dy in OFFSETS:
            for dc in range(2):
                if (dx, dy, dc) != (0, 0, 0):
                    target = chip_at(dx, dy) * 2 + lax.rem(core + dc, 2)
                    pl.semaphore_signal(
                        barrier, inc=1, device_id=(group, target), device_id_type=MESH
                    )

        size = CHIPS * 16
        row = lax.broadcasted_iota(jnp.int32, (size, size), 0)
        col = lax.broadcasted_iota(jnp.int32, (size, size), 1)
        to = row // 16
        item = row % 16
        src_row = ((item % 2) * pieces + (item // 2) % pieces) * heads + to * 2 + item // (2 * pieces)
        send_perm[...] = (col == src_row).astype(jnp.bfloat16)
        tok = row % 32
        src_row = (tok // 2) * 16 + (row // 32) * 2 + tok % 2
        recv_perm[...] = (col == src_row).astype(jnp.bfloat16)

        load_lengths.wait()
        load_cache.wait()
        load_q.wait()

        position = lax.broadcasted_iota(jnp.int32, (heads, positions), 1)
        parts = []
        for r in range(req):
            keys = cache_v[r]
            scores = (
                lax.dot_general(
                    q_v[r], keys, (((1,), (1,)), ((), ())), preferred_element_type=jnp.float32
                )
                * score_scale
            )
            visible = position < lengths_s[r]
            top = jnp.max(jnp.where(visible, scores, -1e30), axis=-1, keepdims=True)
            probs = jnp.exp(jnp.where(visible, scores - top, -1e30))
            total = jnp.sum(probs, axis=-1, keepdims=True)
            summed = jnp.dot(
                probs.astype(jnp.bfloat16), keys[:, :latent], preferred_element_type=jnp.float32
            )
            ctx = (summed / total).astype(jnp.bfloat16)
            for p in range(pieces):
                parts.append(ctx[:, p * LANES : (p + 1) * LANES])
        ctx_send[...] = (
            jnp.dot(
                send_perm[...], jnp.concatenate(parts, axis=0), preferred_element_type=jnp.float32
            )
            .astype(jnp.bfloat16)
            .reshape(CHIPS, 16, LANES)
        )

        load_gain.wait()
        gains = gain_v[...].astype(jnp.float32)
        for k in range(2 * SIDE):
            for i in range(block // LANES):
                at = k * (block // LANES) + i
                gain_f[k, 0:1, i * LANES : (i + 1) * LANES] = gains[at : at + 1, :]

        pl.semaphore_wait(barrier, 2 * CHIPS - 1)

        for dx, dy in OFFSETS:
            for dc in range(2):
                if (dx, dy, dc) != (0, 0, 0):
                    to_chip = chip_at(dx, dy)
                    target = to_chip * 2 + lax.rem(core + dc, 2)
                    copy = remote(
                        ctx_send.at[to_chip], ctx_recv.at[me],
                        ctx_ssem.at[0], ctx_rsem.at[0], target,
                    )
                    copy.start()
        def half_of(which):
            return pl.ds(pl.multiple_of(which * half, LANES), half)

        load_w2 = pltpu.make_async_copy(wout_hbm.at[:, half_of(core)], w2_v.at[core], w2_sem.at[0])
        trade_w2 = remote(
            wout_hbm.at[:, half_of(other)], w2_v.at[core], w2x_send.at[0], w2x_recv.at[0], partner
        )
        load_wuv = pltpu.make_async_copy(wuv_hbm.at[0], wuv_v.at[core], in_sem.at[2])
        trade_wuv = remote(
            wuv_hbm.at[0], wuv_v.at[core], wuvx_send.at[0], wuvx_recv.at[0], partner
        )
        load_hid = pltpu.make_async_copy(
            hid_hbm.at[:, half_of(core)], hid_v.at[core], hid_sem.at[0]
        )
        trade_hid = remote(
            hid_hbm.at[:, half_of(other)], hid_v.at[core], hidx_send.at[0], hidx_recv.at[0], partner
        )
        loads = (load_wuv, load_w2, load_hid)
        trades = (trade_wuv, trade_w2, trade_hid)
        for copy in trades + loads:
            copy.start()
        loads_mlp = []
        for k in range(2 * SIDE):
            for i, (src, dst) in enumerate(((wg_hbm, wg_v), (wu_hbm, wu_v))):
                loads_mlp.append(
                    pltpu.make_async_copy(
                        src.at[:, pl.ds(k * block, block)], dst.at[k], mlp_sem.at[2 * k + i]
                    )
                )
        for copy in loads_mlp:
            copy.start()
        ctx_recv[me] = ctx_send[chip]

        for copy in loads:
            copy.wait()
        for copy in trades:
            copy.wait_recv()
        others = ctx_recv.at[pl.ds(0, 2 * CHIPS - 1)]
        all_ctx = remote(others, others, ctx_ssem.at[0], ctx_rsem.at[0], partner)
        all_ctx.wait_recv()

        got = ctx_recv[...].reshape(2, size, LANES)
        ordered = [
            jnp.dot(recv_perm[...], got[k], preferred_element_type=jnp.float32).astype(jnp.bfloat16)
            for k in range(2)
        ]
        vals = []
        for h in range(2):
            ctx = jnp.concatenate(
                [
                    jnp.concatenate(
                        [o[(h * pieces + p) * 32 : (h * pieces + p + 1) * 32] for p in range(pieces)],
                        axis=1,
                    )
                    for o in ordered
                ],
                axis=0,
            )
            vals.append(
                jnp.dot(ctx, wuv_v[h], preferred_element_type=jnp.float32).astype(jnp.bfloat16)
            )
        vals = jnp.concatenate(vals, axis=1)

        token = lax.broadcasted_iota(jnp.int32, (tokens, block), 0)

        def reduce_copy(piece, dx, dy):
            to_chip = chip_at(dx, dy)
            return remote(
                part_v[piece].at[lax.rem(cx + dx, SIDE), lax.rem(cy + dy, SIDE)],
                red_v[piece].at[chip],
                red_ssem.at[piece], red_rsem.at[piece],
                to_chip * 2 + core,
            )

        def fifteen(piece, ssem, rsem):
            others = red_v[piece].at[pl.ds(0, CHIPS - 1)]
            return remote(others, others, ssem.at[piece], rsem.at[piece], partner)

        for dx in COLUMN_ORDER:
            b = lax.rem(cx + dx, SIDE)
            span = pl.ds(pl.multiple_of(b * block, LANES), block)
            part = jnp.dot(
                vals, w2_v[:, :, span].reshape(2 * value, block), preferred_element_type=jnp.float32
            )
            own = hid_v[:, :, span].astype(jnp.float32)
            for h in range(2):
                for r in range(req):
                    part = part + jnp.where(
                        token == chip * (2 * req) + h * req + r, own[h, r : r + 1, :], 0.0
                    )
            for piece, (low, high) in enumerate(PIECES):
                part_v[piece][b] = (
                    part[:, low:high].astype(jnp.bfloat16).reshape(SIDE, rows, high - low)
                )
            for dy in COLUMN_ORDER:
                if (dx, dy) != (0, 0):
                    reduce_copy(0, dx, dy).start()
        for piece in range(1, len(PIECES)):
            for dx in COLUMN_ORDER:
                for dy in COLUMN_ORDER:
                    if (dx, dy) != (0, 0):
                        reduce_copy(piece, dx, dy).start()
        for part, red in zip(part_v, red_v):
            red[chip] = part[cx, cy]

        for copy in loads_mlp:
            copy.wait()

        def turn(k, carry):
            wg_t[k] = wg_v[k].T
            wu_t[k] = wu_v[k].T
            return carry

        lax.fori_loop(0, 2 * SIDE, turn, 0)
        all_ctx.wait_send()
        for copy in trades:
            copy.wait_send()

        for piece in range(len(PIECES)):
            fifteen(piece, red_ssem, red_rsem).wait_recv()
            total = red_v[piece][0].astype(jnp.float32)
            for k in range(1, CHIPS):
                total = total + red_v[piece][k].astype(jnp.float32)
            x_v[piece][core, cx, cy] = total.astype(jnp.bfloat16)
            for dx, dy in OFFSETS:
                if (dx, dy) != (0, 0):
                    to_chip = chip_at(dx, dy)
                    spot = x_v[piece].at[core, cx, cy]
                    copy = remote(
                        spot, spot, all_ssem.at[piece],
                        all_rsem.at[piece], to_chip * 2 + core,
                    )
                    copy.start()

        def multiply(which, b, piece, carry):
            low, high = PIECES[piece]
            gate, up, square = carry
            k = which * SIDE + b
            x = x_v[piece][which, b].reshape(tokens, high - low).astype(jnp.float32)
            square = square + jnp.sum(x * x, axis=-1, keepdims=True)
            x = (x * gain_f[k, :, low:high]).astype(jnp.bfloat16)
            gate = gate + jnp.dot(x, wg_t[k, low:high, :], preferred_element_type=jnp.float32)
            up = up + jnp.dot(x, wu_t[k, low:high, :], preferred_element_type=jnp.float32)
            return (gate, up, square)

        carry = (
            jnp.zeros((tokens, hidden), jnp.float32),
            jnp.zeros((tokens, hidden), jnp.float32),
            jnp.zeros((tokens, 1), jnp.float32),
        )
        def forward(piece, which):
            spot = x_v[piece].at[which]
            return remote(spot, spot, fwd_ssem.at[piece], fwd_rsem.at[piece], partner)

        def own_blocks(piece, carry):
            fifteen(piece, all_ssem, all_rsem).wait_recv()
            forward(piece, core).start()
            for b in range(SIDE):
                carry = multiply(core, b, piece, carry)
            return carry

        def partner_blocks(piece, carry):
            forward(piece, other).wait_recv()
            for b in range(SIDE):
                carry = multiply(other, b, piece, carry)
            return carry

        first = lax.rem(chip, SIDE) * (2 * req) + core * req

        def keep_rows(which, piece):
            low, high = PIECES[piece]
            line = lax.broadcasted_iota(jnp.int32, (rows, high - low), 0)
            for b in range(SIDE):
                x = x_v[piece][which, b, cy].astype(jnp.float32)
                picked = [
                    jnp.sum(jnp.where(line == first + r, x, 0.0), axis=0, keepdims=True)
                    for r in range(req)
                ]
                at = pl.multiple_of(which * half + b * block + low, LANES)
                att_ref[:, pl.ds(at, high - low)] = jnp.concatenate(picked, axis=0).astype(
                    jnp.bfloat16
                )

        for piece in range(len(PIECES)):
            fifteen(piece, red_ssem, red_rsem).wait_send()
        last = len(PIECES) - 1
        for piece in range(last + 1):
            carry = own_blocks(piece, carry)
            if piece > 0:
                carry = partner_blocks(piece - 1, carry)
                keep_rows(other, piece - 1)
            keep_rows(core, piece)
        carry = partner_blocks(last, carry)
        gate, up, square = carry
        scale = lax.rsqrt(square / width + 1e-6)
        gate = gate * scale
        up = up * scale
        mlp_ref[...] = (gate / (1.0 + jnp.exp(-gate)) * up).astype(jnp.bfloat16)

        keep_rows(other, last)

        for piece in range(len(PIECES)):
            fifteen(piece, all_ssem, red_rsem).wait_send()
        for piece in range(len(PIECES)):
            forward(piece, core).wait_send()

    return kernel


def write_out(att_ref, mlp_ref, att_hbm, mlp_hbm, sem):
    copies = (
        pltpu.make_async_copy(att_ref, att_hbm, sem.at[0]),
        pltpu.make_async_copy(mlp_ref, mlp_hbm, sem.at[1]),
    )
    for copy in copies:
        copy.start()
    for copy in copies:
        copy.wait()


def per_device(hidden_in, queries, cache, lengths, w_uv, w_out, norm_gain, w_gate, w_up):
    req, heads, depth = queries.shape
    positions = cache.shape[1]
    latent, value = w_uv.shape[1:]
    width, hidden = w_gate.shape
    rotary = depth - latent
    tokens = req * 2 * CHIPS
    half = width // 2
    block = half // SIDE
    rows = tokens // SIDE
    size = CHIPS * 16
    bf16 = jnp.bfloat16
    dma = pltpu.SemaphoreType.DMA
    hbm = pl.BlockSpec(memory_space=pltpu.HBM)
    vmem = pl.BlockSpec(memory_space=pltpu.VMEM)
    outs = (
        jax.ShapeDtypeStruct((req, width), bf16),
        jax.ShapeDtypeStruct((tokens, hidden), bf16),
    )
    att, mlp = pl.pallas_call(
        make_kernel(req, heads, latent, value, rotary, width, hidden, positions),
        out_shape=outs,
        in_specs=[hbm] * 9,
        out_specs=(vmem, vmem),
        scratch_shapes=[
            pltpu.SMEM((req,), jnp.int32),
            pltpu.VMEM((req, heads, depth), bf16),
            pltpu.VMEM((req, positions, depth), bf16),
            pltpu.VMEM((2, latent, value), bf16),
            pltpu.VMEM((2, value, half), bf16),
            pltpu.VMEM((2, req, half), bf16),
            pltpu.VMEM((width // LANES, LANES), bf16),
            pltpu.VMEM((2 * SIDE, 1, block), jnp.float32),
            pltpu.VMEM((2 * SIDE, hidden, block), bf16),
            pltpu.VMEM((2 * SIDE, hidden, block), bf16),
            pltpu.VMEM((2 * SIDE, block, hidden), bf16),
            pltpu.VMEM((2 * SIDE, block, hidden), bf16),
            pltpu.VMEM((size, size), bf16),
            pltpu.VMEM((size, size), bf16),
            pltpu.VMEM((CHIPS, 16, LANES), bf16),
            pltpu.VMEM((2 * CHIPS, 16, LANES), bf16),
            [pltpu.VMEM((SIDE, SIDE, rows, high - low), bf16) for low, high in PIECES],
            [pltpu.VMEM((CHIPS, rows, high - low), bf16) for low, high in PIECES],
            [pltpu.VMEM((2, SIDE, SIDE, rows, high - low), bf16) for low, high in PIECES],
            dma((5,)),
            dma((1,)),
            dma((1,)),
            dma((4 * SIDE,)),
            dma((1,)),
            dma((1,)),
            dma((1,)),
            dma((1,)),
            dma((1,)),
            dma((1,)),
            dma((1,)),
            dma((1,)),
            dma((len(PIECES),)),
            dma((len(PIECES),)),
            dma((len(PIECES),)),
            dma((len(PIECES),)),
            dma((len(PIECES),)),
            dma((len(PIECES),)),
        ],
        compiler_params=pltpu.CompilerParams(
            collective_id=0, has_side_effects=True, vmem_limit_bytes=40 * 1024 * 1024
        ),
    )(
        *(
            pltpu.with_memory_space_constraint(operand, pltpu.HBM)
            for operand in (
                lengths, hidden_in, queries, cache, w_uv, w_out,
                norm_gain.reshape(width // LANES, LANES), w_gate.T, w_up.T,
            )
        )
    )
    return pl.pallas_call(
        write_out,
        out_shape=outs,
        in_specs=[vmem, vmem],
        out_specs=(hbm, hbm),
        scratch_shapes=[dma((2,))],
        compiler_params=pltpu.CompilerParams(vmem_limit_bytes=1024 * 1024),
    )(att, mlp)


def solution(mesh):
    in_specs = (
        P(("group", "tp"), None),
        P(("group", "tp"), None, None),
        P(("group", "tp"), None, None),
        P(("group", "tp")),
        P("tp", None, None),
        P("tp", None),
        P(),
        P(None, "tp"),
        P(None, "tp"),
    )
    out_specs = (P(("group", "tp"), None), P("group", "tp"))
    return jax.shard_map(
        per_device, mesh=mesh, in_specs=in_specs, out_specs=out_specs, check_vma=False
    )
```

```python
import math

import jax
import jax.numpy as jnp
from jax import lax
from jax.experimental import pallas as pl
from jax.experimental.pallas import tpu as pltpu
from jax.sharding import PartitionSpec as P

MESH = pl.DeviceIdType.MESH
SIDE = 4
CHIPS = SIDE * SIDE
LANES = 128
OFFSETS = sorted(
    ((dx, dy) for dx in range(SIDE) for dy in range(SIDE)),
    key=lambda o: -(min(o[0], SIDE - o[0]) + min(o[1], SIDE - o[1])),
)
COLUMN_ORDER = (2, 1, 3, 0)
PIECES = ((0, 256), (256, 512), (512, 768), (768, 896))


def make_kernel(req, heads, latent, value, rotary, width, hidden, positions):
    tokens = req * 2 * CHIPS
    half = width // 2
    block = half // SIDE
    rows = tokens // SIDE
    score_scale = 1.0 / math.sqrt(value + rotary)
    pieces = latent // LANES

    def kernel(
        lengths_hbm, hid_hbm, q_hbm, cache_hbm, wuv_hbm, wout_hbm, gain_hbm, wg_hbm, wu_hbm,
        att_ref, mlp_ref,
        lengths_s, q_v, cache_v, wuv_v, w2_v, hid_v, gain_v, gain_f, wg_v, wu_v, wg_t, wu_t, send_perm, recv_perm,
        ctx_send, ctx_recv, part_v, red_v, x_v,
        in_sem, w2_sem, hid_sem, mlp_sem, w2x_send, w2x_recv, hidx_send, hidx_recv, wuvx_send, wuvx_recv,
        ctx_ssem, ctx_rsem, red_ssem, red_rsem, all_ssem, all_rsem, fwd_ssem, fwd_rsem,
    ):
        group = lax.axis_index("group")
        me = lax.axis_index("tp")
        core = lax.rem(me, 2)
        other = 1 - core
        chip = me // 2
        cx = lax.rem(chip, SIDE)
        cy = chip // SIDE

        def chip_at(dx, dy):
            return lax.rem(cy + dy, SIDE) * SIDE + lax.rem(cx + dx, SIDE)

        def remote(src, dst, ssem, rsem, target):
            return pltpu.make_async_remote_copy(
                src_ref=src, dst_ref=dst, send_sem=ssem, recv_sem=rsem,
                device_id=(group, target), device_id_type=MESH,
            )

        partner = chip * 2 + other

        load_cache = pltpu.make_async_copy(cache_hbm, cache_v, in_sem.at[0])
        load_q = pltpu.make_async_copy(q_hbm, q_v, in_sem.at[1])
        load_lengths = pltpu.make_async_copy(lengths_hbm, lengths_s, in_sem.at[3])
        load_gain = pltpu.make_async_copy(gain_hbm, gain_v, in_sem.at[4])
        load_cache.start()
        load_q.start()
        load_lengths.start()
        load_gain.start()
        barrier = pltpu.get_barrier_semaphore()
        for dx, dy in OFFSETS:
            for dc in range(2):
                if (dx, dy, dc) != (0, 0, 0):
                    target = chip_at(dx, dy) * 2 + lax.rem(core + dc, 2)
                    pl.semaphore_signal(
                        barrier, inc=1, device_id=(group, target), device_id_type=MESH
                    )

        size = CHIPS * 16
        row = lax.broadcasted_iota(jnp.int32, (size, size), 0)
        col = lax.broadcasted_iota(jnp.int32, (size, size), 1)
        to = row // 16
        item = row % 16
        src_row = ((item % 2) * pieces + (item // 2) % pieces) * heads + to * 2 + item // (2 * pieces)
        send_perm[...] = (col == src_row).astype(jnp.bfloat16)
        tok = row % 32
        src_row = (tok // 2) * 16 + (row // 32) * 2 + tok % 2
        recv_perm[...] = (col == src_row).astype(jnp.bfloat16)

        load_lengths.wait()
        load_cache.wait()
        load_q.wait()

        position = lax.broadcasted_iota(jnp.int32, (heads, positions), 1)
        parts = []
        for r in range(req):
            keys = cache_v[r]
            scores = (
                lax.dot_general(
                    q_v[r], keys, (((1,), (1,)), ((), ())), preferred_element_type=jnp.float32
                )
                * score_scale
            )
            visible = position < lengths_s[r]
            top = jnp.max(jnp.where(visible, scores, -1e30), axis=-1, keepdims=True)
            probs = jnp.exp(jnp.where(visible, scores - top, -1e30))
            total = jnp.sum(probs, axis=-1, keepdims=True)
            summed = jnp.dot(
                probs.astype(jnp.bfloat16), keys[:, :latent], preferred_element_type=jnp.float32
            )
            ctx = (summed / total).astype(jnp.bfloat16)
            for p in range(pieces):
                parts.append(ctx[:, p * LANES : (p + 1) * LANES])
        ctx_send[...] = (
            jnp.dot(
                send_perm[...], jnp.concatenate(parts, axis=0), preferred_element_type=jnp.float32
            )
            .astype(jnp.bfloat16)
            .reshape(CHIPS, 16, LANES)
        )

        load_gain.wait()
        gains = gain_v[...].astype(jnp.float32)
        for k in range(2 * SIDE):
            for i in range(block // LANES):
                at = k * (block // LANES) + i
                gain_f[k, 0:1, i * LANES : (i + 1) * LANES] = gains[at : at + 1, :]

        pl.semaphore_wait(barrier, 2 * CHIPS - 1)

        for dx, dy in OFFSETS:
            for dc in range(2):
                if (dx, dy, dc) != (0, 0, 0):
                    to_chip = chip_at(dx, dy)
                    target = to_chip * 2 + lax.rem(core + dc, 2)
                    copy = remote(
                        ctx_send.at[to_chip], ctx_recv.at[me],
                        ctx_ssem.at[0], ctx_rsem.at[0], target,
                    )
                    copy.start()
        def half_of(which):
            return pl.ds(pl.multiple_of(which * half, LANES), half)

        load_w2 = pltpu.make_async_copy(wout_hbm.at[:, half_of(core)], w2_v.at[core], w2_sem.at[0])
        trade_w2 = remote(
            wout_hbm.at[:, half_of(other)], w2_v.at[core], w2x_send.at[0], w2x_recv.at[0], partner
        )
        load_wuv = pltpu.make_async_copy(wuv_hbm.at[0], wuv_v.at[core], in_sem.at[2])
        trade_wuv = remote(
            wuv_hbm.at[0], wuv_v.at[core], wuvx_send.at[0], wuvx_recv.at[0], partner
        )
        load_hid = pltpu.make_async_copy(
            hid_hbm.at[:, half_of(core)], hid_v.at[core], hid_sem.at[0]
        )
        trade_hid = remote(
            hid_hbm.at[:, half_of(other)], hid_v.at[core], hidx_send.at[0], hidx_recv.at[0], partner
        )
        loads = (load_wuv, load_w2, load_hid)
        trades = (trade_wuv, trade_w2, trade_hid)
        for copy in trades + loads:
            copy.start()
        loads_mlp = []
        for k in range(2 * SIDE):
            for i, (src, dst) in enumerate(((wg_hbm, wg_v), (wu_hbm, wu_v))):
                loads_mlp.append(
                    pltpu.make_async_copy(
                        src.at[:, pl.ds(k * block, block)], dst.at[k], mlp_sem.at[2 * k + i]
                    )
                )
        for copy in loads_mlp:
            copy.start()
        ctx_recv[me] = ctx_send[chip]

        for copy in loads:
            copy.wait()
        for copy in trades:
            copy.wait_recv()
        others = ctx_recv.at[pl.ds(0, 2 * CHIPS - 1)]
        all_ctx = remote(others, others, ctx_ssem.at[0], ctx_rsem.at[0], partner)
        all_ctx.wait_recv()

        got = ctx_recv[...].reshape(2, size, LANES)
        ordered = [
            jnp.dot(recv_perm[...], got[k], preferred_element_type=jnp.float32).astype(jnp.bfloat16)
            for k in range(2)
        ]
        vals = []
        for h in range(2):
            ctx = jnp.concatenate(
                [
                    jnp.concatenate(
                        [o[(h * pieces + p) * 32 : (h * pieces + p + 1) * 32] for p in range(pieces)],
                        axis=1,
                    )
                    for o in ordered
                ],
                axis=0,
            )
            vals.append(
                jnp.dot(ctx, wuv_v[h], preferred_element_type=jnp.float32).astype(jnp.bfloat16)
            )
        vals = jnp.concatenate(vals, axis=1)

        token = lax.broadcasted_iota(jnp.int32, (tokens, block), 0)

        def reduce_copy(piece, dx, dy):
            to_chip = chip_at(dx, dy)
            return remote(
                part_v[piece].at[lax.rem(cx + dx, SIDE), lax.rem(cy + dy, SIDE)],
                red_v[piece].at[chip],
                red_ssem.at[piece], red_rsem.at[piece],
                to_chip * 2 + core,
            )

        def fifteen(piece, ssem, rsem):
            others = red_v[piece].at[pl.ds(0, CHIPS - 1)]
            return remote(others, others, ssem.at[piece], rsem.at[piece], partner)

        for dx in COLUMN_ORDER:
            b = lax.rem(cx + dx, SIDE)
            span = pl.ds(pl.multiple_of(b * block, LANES), block)
            part = jnp.dot(
                vals, w2_v[:, :, span].reshape(2 * value, block), preferred_element_type=jnp.float32
            )
            own = hid_v[:, :, span].astype(jnp.float32)
            for h in range(2):
                for r in range(req):
                    part = part + jnp.where(
                        token == chip * (2 * req) + h * req + r, own[h, r : r + 1, :], 0.0
                    )
            for piece, (low, high) in enumerate(PIECES):
                part_v[piece][b] = (
                    part[:, low:high].astype(jnp.bfloat16).reshape(SIDE, rows, high - low)
                )
            for dy in COLUMN_ORDER:
                if (dx, dy) != (0, 0):
                    reduce_copy(0, dx, dy).start()
        for piece in range(1, len(PIECES)):
            for dx in COLUMN_ORDER:
                for dy in COLUMN_ORDER:
                    if (dx, dy) != (0, 0):
                        reduce_copy(piece, dx, dy).start()
        for part, red in zip(part_v, red_v):
            red[chip] = part[cx, cy]

        for copy in loads_mlp:
            copy.wait()

        def turn(k, carry):
            wg_t[k] = wg_v[k].T
            wu_t[k] = wu_v[k].T
            return carry

        lax.fori_loop(0, 2 * SIDE, turn, 0)
        all_ctx.wait_send()
        for copy in trades:
            copy.wait_send()

        for piece in range(len(PIECES)):
            fifteen(piece, red_ssem, red_rsem).wait_recv()
            total = red_v[piece][0].astype(jnp.float32)
            for k in range(1, CHIPS):
                total = total + red_v[piece][k].astype(jnp.float32)
            x_v[piece][core, cx, cy] = total.astype(jnp.bfloat16)
            for dx, dy in OFFSETS:
                if (dx, dy) != (0, 0):
                    to_chip = chip_at(dx, dy)
                    spot = x_v[piece].at[core, cx, cy]
                    copy = remote(
                        spot, spot, all_ssem.at[piece],
                        all_rsem.at[piece], to_chip * 2 + core,
                    )
                    copy.start()
            if piece == len(PIECES) - 1:
                for dx, dy in OFFSETS:
                    spot = x_v[piece].at[core, cx, cy]
                    remote(
                        spot, spot, fwd_ssem.at[piece], fwd_rsem.at[piece],
                        chip_at(dx, dy) * 2 + other,
                    ).start()

        def multiply(which, b, piece, carry):
            low, high = PIECES[piece]
            gate, up, square = carry
            k = which * SIDE + b
            x = x_v[piece][which, b].reshape(tokens, high - low).astype(jnp.float32)
            square = square + jnp.sum(x * x, axis=-1, keepdims=True)
            x = (x * gain_f[k, :, low:high]).astype(jnp.bfloat16)
            gate = gate + jnp.dot(x, wg_t[k, low:high, :], preferred_element_type=jnp.float32)
            up = up + jnp.dot(x, wu_t[k, low:high, :], preferred_element_type=jnp.float32)
            return (gate, up, square)

        carry = (
            jnp.zeros((tokens, hidden), jnp.float32),
            jnp.zeros((tokens, hidden), jnp.float32),
            jnp.zeros((tokens, 1), jnp.float32),
        )
        def forward(piece, which):
            spot = x_v[piece].at[which]
            return remote(spot, spot, fwd_ssem.at[piece], fwd_rsem.at[piece], partner)

        def own_blocks(piece, carry):
            fifteen(piece, all_ssem, all_rsem).wait_recv()
            if piece < len(PIECES) - 1:
                forward(piece, core).start()
            for b in range(SIDE):
                carry = multiply(core, b, piece, carry)
            return carry

        def partner_blocks(piece, carry):
            forward(piece, other).wait_recv()
            for b in range(SIDE):
                carry = multiply(other, b, piece, carry)
            return carry

        first = lax.rem(chip, SIDE) * (2 * req) + core * req

        def keep_rows(which, piece):
            low, high = PIECES[piece]
            line = lax.broadcasted_iota(jnp.int32, (rows, high - low), 0)
            for b in range(SIDE):
                x = x_v[piece][which, b, cy].astype(jnp.float32)
                picked = [
                    jnp.sum(jnp.where(line == first + r, x, 0.0), axis=0, keepdims=True)
                    for r in range(req)
                ]
                at = pl.multiple_of(which * half + b * block + low, LANES)
                att_ref[:, pl.ds(at, high - low)] = jnp.concatenate(picked, axis=0).astype(
                    jnp.bfloat16
                )

        for piece in range(len(PIECES)):
            fifteen(piece, red_ssem, red_rsem).wait_send()
        last = len(PIECES) - 1
        for piece in range(last + 1):
            carry = own_blocks(piece, carry)
            if piece > 0:
                carry = partner_blocks(piece - 1, carry)
                keep_rows(other, piece - 1)
            keep_rows(core, piece)
        carry = partner_blocks(last, carry)
        gate, up, square = carry
        scale = lax.rsqrt(square / width + 1e-6)
        gate = gate * scale
        up = up * scale
        mlp_ref[...] = (gate / (1.0 + jnp.exp(-gate)) * up).astype(jnp.bfloat16)

        keep_rows(other, last)

        for piece in range(len(PIECES)):
            fifteen(piece, all_ssem, red_rsem).wait_send()
        for piece in range(len(PIECES)):
            forward(piece, core).wait_send()

    return kernel


def write_out(att_ref, mlp_ref, att_hbm, mlp_hbm, sem):
    copies = (
        pltpu.make_async_copy(att_ref, att_hbm, sem.at[0]),
        pltpu.make_async_copy(mlp_ref, mlp_hbm, sem.at[1]),
    )
    for copy in copies:
        copy.start()
    for copy in copies:
        copy.wait()


def per_device(hidden_in, queries, cache, lengths, w_uv, w_out, norm_gain, w_gate, w_up):
    req, heads, depth = queries.shape
    positions = cache.shape[1]
    latent, value = w_uv.shape[1:]
    width, hidden = w_gate.shape
    rotary = depth - latent
    tokens = req * 2 * CHIPS
    half = width // 2
    block = half // SIDE
    rows = tokens // SIDE
    size = CHIPS * 16
    bf16 = jnp.bfloat16
    dma = pltpu.SemaphoreType.DMA
    hbm = pl.BlockSpec(memory_space=pltpu.HBM)
    vmem = pl.BlockSpec(memory_space=pltpu.VMEM)
    outs = (
        jax.ShapeDtypeStruct((req, width), bf16),
        jax.ShapeDtypeStruct((tokens, hidden), bf16),
    )
    att, mlp = pl.pallas_call(
        make_kernel(req, heads, latent, value, rotary, width, hidden, positions),
        out_shape=outs,
        in_specs=[hbm] * 9,
        out_specs=(vmem, vmem),
        scratch_shapes=[
            pltpu.SMEM((req,), jnp.int32),
            pltpu.VMEM((req, heads, depth), bf16),
            pltpu.VMEM((req, positions, depth), bf16),
            pltpu.VMEM((2, latent, value), bf16),
            pltpu.VMEM((2, value, half), bf16),
            pltpu.VMEM((2, req, half), bf16),
            pltpu.VMEM((width // LANES, LANES), bf16),
            pltpu.VMEM((2 * SIDE, 1, block), jnp.float32),
            pltpu.VMEM((2 * SIDE, hidden, block), bf16),
            pltpu.VMEM((2 * SIDE, hidden, block), bf16),
            pltpu.VMEM((2 * SIDE, block, hidden), bf16),
            pltpu.VMEM((2 * SIDE, block, hidden), bf16),
            pltpu.VMEM((size, size), bf16),
            pltpu.VMEM((size, size), bf16),
            pltpu.VMEM((CHIPS, 16, LANES), bf16),
            pltpu.VMEM((2 * CHIPS, 16, LANES), bf16),
            [pltpu.VMEM((SIDE, SIDE, rows, high - low), bf16) for low, high in PIECES],
            [pltpu.VMEM((CHIPS, rows, high - low), bf16) for low, high in PIECES],
            [pltpu.VMEM((2, SIDE, SIDE, rows, high - low), bf16) for low, high in PIECES],
            dma((5,)),
            dma((1,)),
            dma((1,)),
            dma((4 * SIDE,)),
            dma((1,)),
            dma((1,)),
            dma((1,)),
            dma((1,)),
            dma((1,)),
            dma((1,)),
            dma((1,)),
            dma((1,)),
            dma((len(PIECES),)),
            dma((len(PIECES),)),
            dma((len(PIECES),)),
            dma((len(PIECES),)),
            dma((len(PIECES),)),
            dma((len(PIECES),)),
        ],
        compiler_params=pltpu.CompilerParams(
            collective_id=0, has_side_effects=True, vmem_limit_bytes=40 * 1024 * 1024
        ),
    )(
        *(
            pltpu.with_memory_space_constraint(operand, pltpu.HBM)
            for operand in (
                lengths, hidden_in, queries, cache, w_uv, w_out,
                norm_gain.reshape(width // LANES, LANES), w_gate.T, w_up.T,
            )
        )
    )
    return pl.pallas_call(
        write_out,
        out_shape=outs,
        in_specs=[vmem, vmem],
        out_specs=(hbm, hbm),
        scratch_shapes=[dma((2,))],
        compiler_params=pltpu.CompilerParams(vmem_limit_bytes=1024 * 1024),
    )(att, mlp)


def solution(mesh):
    in_specs = (
        P(("group", "tp"), None),
        P(("group", "tp"), None, None),
        P(("group", "tp"), None, None),
        P(("group", "tp")),
        P("tp", None, None),
        P("tp", None),
        P(),
        P(None, "tp"),
        P(None, "tp"),
    )
    out_specs = (P(("group", "tp"), None), P("group", "tp"))
    return jax.shard_map(
        per_device, mesh=mesh, in_specs=in_specs, out_specs=out_specs, check_vma=False
    )
```

```python
import math

import jax
import jax.numpy as jnp
from jax import lax
from jax.experimental import pallas as pl
from jax.experimental.pallas import tpu as pltpu
from jax.sharding import PartitionSpec as P

MESH = pl.DeviceIdType.MESH
SIDE = 4
CHIPS = SIDE * SIDE
LANES = 128
OFFSETS = sorted(
    ((dx, dy) for dx in range(SIDE) for dy in range(SIDE)),
    key=lambda o: -(min(o[0], SIDE - o[0]) + min(o[1], SIDE - o[1])),
)
COLUMN_ORDER = (2, 1, 3, 0)
PIECES = ((0, 384), (384, 768), (768, 896))


def make_kernel(req, heads, latent, value, rotary, width, hidden, positions):
    tokens = req * 2 * CHIPS
    half = width // 2
    block = half // SIDE
    rows = tokens // SIDE
    score_scale = 1.0 / math.sqrt(value + rotary)
    pieces = latent // LANES

    def kernel(
        lengths_hbm, hid_hbm, q_hbm, cache_hbm, wuv_hbm, wout_hbm, gain_hbm, wg_hbm, wu_hbm,
        att_ref, mlp_ref,
        lengths_s, q_v, cache_v, wuv_v, w2_v, hid_v, gain_v, gain_f, wg_v, wu_v, wg_t, wu_t, send_perm, recv_perm,
        ctx_send, ctx_recv, part_v, red_v, x_v,
        in_sem, w2_sem, hid_sem, mlp_sem, w2x_send, w2x_recv, hidx_send, hidx_recv, wuvx_send, wuvx_recv,
        ctx_ssem, ctx_rsem, red_ssem, red_rsem, all_ssem, all_rsem, fwd_ssem, fwd_rsem,
    ):
        group = lax.axis_index("group")
        me = lax.axis_index("tp")
        core = lax.rem(me, 2)
        other = 1 - core
        chip = me // 2
        cx = lax.rem(chip, SIDE)
        cy = chip // SIDE

        def chip_at(dx, dy):
            return lax.rem(cy + dy, SIDE) * SIDE + lax.rem(cx + dx, SIDE)

        def remote(src, dst, ssem, rsem, target):
            return pltpu.make_async_remote_copy(
                src_ref=src, dst_ref=dst, send_sem=ssem, recv_sem=rsem,
                device_id=(group, target), device_id_type=MESH,
            )

        partner = chip * 2 + other

        load_cache = pltpu.make_async_copy(cache_hbm, cache_v, in_sem.at[0])
        load_q = pltpu.make_async_copy(q_hbm, q_v, in_sem.at[1])
        load_lengths = pltpu.make_async_copy(lengths_hbm, lengths_s, in_sem.at[3])
        load_gain = pltpu.make_async_copy(gain_hbm, gain_v, in_sem.at[4])
        load_cache.start()
        load_q.start()
        load_lengths.start()
        load_gain.start()
        barrier = pltpu.get_barrier_semaphore()
        for dx, dy in OFFSETS:
            for dc in range(2):
                if (dx, dy, dc) != (0, 0, 0):
                    target = chip_at(dx, dy) * 2 + lax.rem(core + dc, 2)
                    pl.semaphore_signal(
                        barrier, inc=1, device_id=(group, target), device_id_type=MESH
                    )

        size = CHIPS * 16
        row = lax.broadcasted_iota(jnp.int32, (size, size), 0)
        col = lax.broadcasted_iota(jnp.int32, (size, size), 1)
        to = row // 16
        item = row % 16
        src_row = ((item % 2) * pieces + (item // 2) % pieces) * heads + to * 2 + item // (2 * pieces)
        send_perm[...] = (col == src_row).astype(jnp.bfloat16)
        tok = row % 32
        src_row = (tok // 2) * 16 + (row // 32) * 2 + tok % 2
        recv_perm[...] = (col == src_row).astype(jnp.bfloat16)

        load_lengths.wait()
        load_cache.wait()
        load_q.wait()

        position = lax.broadcasted_iota(jnp.int32, (heads, positions), 1)
        parts = []
        for r in range(req):
            keys = cache_v[r]
            scores = (
                lax.dot_general(
                    q_v[r], keys, (((1,), (1,)), ((), ())), preferred_element_type=jnp.float32
                )
                * score_scale
            )
            visible = position < lengths_s[r]
            top = jnp.max(jnp.where(visible, scores, -1e30), axis=-1, keepdims=True)
            probs = jnp.exp(jnp.where(visible, scores - top, -1e30))
            total = jnp.sum(probs, axis=-1, keepdims=True)
            summed = jnp.dot(
                probs.astype(jnp.bfloat16), keys[:, :latent], preferred_element_type=jnp.float32
            )
            ctx = (summed / total).astype(jnp.bfloat16)
            for p in range(pieces):
                parts.append(ctx[:, p * LANES : (p + 1) * LANES])
        ctx_send[...] = (
            jnp.dot(
                send_perm[...], jnp.concatenate(parts, axis=0), preferred_element_type=jnp.float32
            )
            .astype(jnp.bfloat16)
            .reshape(CHIPS, 16, LANES)
        )

        load_gain.wait()
        gains = gain_v[...].astype(jnp.float32)
        for k in range(2 * SIDE):
            for i in range(block // LANES):
                at = k * (block // LANES) + i
                gain_f[k, 0:1, i * LANES : (i + 1) * LANES] = gains[at : at + 1, :]

        pl.semaphore_wait(barrier, 2 * CHIPS - 1)

        for dx, dy in OFFSETS:
            for dc in range(2):
                if (dx, dy, dc) != (0, 0, 0):
                    to_chip = chip_at(dx, dy)
                    target = to_chip * 2 + lax.rem(core + dc, 2)
                    copy = remote(
                        ctx_send.at[to_chip], ctx_recv.at[me],
                        ctx_ssem.at[0], ctx_rsem.at[0], target,
                    )
                    copy.start()
        def half_of(which):
            return pl.ds(pl.multiple_of(which * half, LANES), half)

        load_w2 = pltpu.make_async_copy(wout_hbm.at[:, half_of(core)], w2_v.at[core], w2_sem.at[0])
        trade_w2 = remote(
            wout_hbm.at[:, half_of(other)], w2_v.at[core], w2x_send.at[0], w2x_recv.at[0], partner
        )
        load_wuv = pltpu.make_async_copy(wuv_hbm.at[0], wuv_v.at[core], in_sem.at[2])
        trade_wuv = remote(
            wuv_hbm.at[0], wuv_v.at[core], wuvx_send.at[0], wuvx_recv.at[0], partner
        )
        load_hid = pltpu.make_async_copy(
            hid_hbm.at[:, half_of(core)], hid_v.at[core], hid_sem.at[0]
        )
        trade_hid = remote(
            hid_hbm.at[:, half_of(other)], hid_v.at[core], hidx_send.at[0], hidx_recv.at[0], partner
        )
        loads = (load_wuv, load_w2, load_hid)
        trades = (trade_wuv, trade_w2, trade_hid)
        for copy in trades + loads:
            copy.start()
        loads_mlp = []
        for k in range(2 * SIDE):
            for i, (src, dst) in enumerate(((wg_hbm, wg_v), (wu_hbm, wu_v))):
                loads_mlp.append(
                    pltpu.make_async_copy(
                        src.at[:, pl.ds(k * block, block)], dst.at[k], mlp_sem.at[2 * k + i]
                    )
                )
        for copy in loads_mlp:
            copy.start()
        ctx_recv[me] = ctx_send[chip]

        for copy in loads:
            copy.wait()
        for copy in trades:
            copy.wait_recv()
        others = ctx_recv.at[pl.ds(0, 2 * CHIPS - 1)]
        all_ctx = remote(others, others, ctx_ssem.at[0], ctx_rsem.at[0], partner)
        all_ctx.wait_recv()

        got = ctx_recv[...].reshape(2, size, LANES)
        ordered = [
            jnp.dot(recv_perm[...], got[k], preferred_element_type=jnp.float32).astype(jnp.bfloat16)
            for k in range(2)
        ]
        vals = []
        for h in range(2):
            ctx = jnp.concatenate(
                [
                    jnp.concatenate(
                        [o[(h * pieces + p) * 32 : (h * pieces + p + 1) * 32] for p in range(pieces)],
                        axis=1,
                    )
                    for o in ordered
                ],
                axis=0,
            )
            vals.append(
                jnp.dot(ctx, wuv_v[h], preferred_element_type=jnp.float32).astype(jnp.bfloat16)
            )
        vals = jnp.concatenate(vals, axis=1)

        token = lax.broadcasted_iota(jnp.int32, (tokens, block), 0)

        def reduce_copy(piece, dx, dy):
            to_chip = chip_at(dx, dy)
            return remote(
                part_v[piece].at[lax.rem(cx + dx, SIDE), lax.rem(cy + dy, SIDE)],
                red_v[piece].at[chip],
                red_ssem.at[piece], red_rsem.at[piece],
                to_chip * 2 + core,
            )

        def fifteen(piece, ssem, rsem):
            others = red_v[piece].at[pl.ds(0, CHIPS - 1)]
            return remote(others, others, ssem.at[piece], rsem.at[piece], partner)

        for dx in COLUMN_ORDER:
            b = lax.rem(cx + dx, SIDE)
            span = pl.ds(pl.multiple_of(b * block, LANES), block)
            part = jnp.dot(
                vals, w2_v[:, :, span].reshape(2 * value, block), preferred_element_type=jnp.float32
            )
            own = hid_v[:, :, span].astype(jnp.float32)
            for h in range(2):
                for r in range(req):
                    part = part + jnp.where(
                        token == chip * (2 * req) + h * req + r, own[h, r : r + 1, :], 0.0
                    )
            for piece, (low, high) in enumerate(PIECES):
                part_v[piece][b] = (
                    part[:, low:high].astype(jnp.bfloat16).reshape(SIDE, rows, high - low)
                )
            for dy in COLUMN_ORDER:
                if (dx, dy) != (0, 0):
                    reduce_copy(0, dx, dy).start()
        for piece in range(1, len(PIECES)):
            for dx in COLUMN_ORDER:
                for dy in COLUMN_ORDER:
                    if (dx, dy) != (0, 0):
                        reduce_copy(piece, dx, dy).start()
        for part, red in zip(part_v, red_v):
            red[chip] = part[cx, cy]

        for copy in loads_mlp:
            copy.wait()

        def turn(k, carry):
            wg_t[k] = wg_v[k].T
            wu_t[k] = wu_v[k].T
            return carry

        lax.fori_loop(0, 2 * SIDE, turn, 0)
        all_ctx.wait_send()
        for copy in trades:
            copy.wait_send()

        for piece in range(len(PIECES)):
            fifteen(piece, red_ssem, red_rsem).wait_recv()
            total = red_v[piece][0].astype(jnp.float32)
            for k in range(1, CHIPS):
                total = total + red_v[piece][k].astype(jnp.float32)
            x_v[piece][core, cx, cy] = total.astype(jnp.bfloat16)
            for dx, dy in OFFSETS:
                if (dx, dy) != (0, 0):
                    to_chip = chip_at(dx, dy)
                    spot = x_v[piece].at[core, cx, cy]
                    copy = remote(
                        spot, spot, all_ssem.at[piece],
                        all_rsem.at[piece], to_chip * 2 + core,
                    )
                    copy.start()
            if piece == len(PIECES) - 1:
                for dx, dy in OFFSETS:
                    spot = x_v[piece].at[core, cx, cy]
                    remote(
                        spot, spot, fwd_ssem.at[piece], fwd_rsem.at[piece],
                        chip_at(dx, dy) * 2 + other,
                    ).start()

        def multiply(which, b, piece, carry):
            low, high = PIECES[piece]
            gate, up, square = carry
            k = which * SIDE + b
            x = x_v[piece][which, b].reshape(tokens, high - low).astype(jnp.float32)
            square = square + jnp.sum(x * x, axis=-1, keepdims=True)
            x = (x * gain_f[k, :, low:high]).astype(jnp.bfloat16)
            gate = gate + jnp.dot(x, wg_t[k, low:high, :], preferred_element_type=jnp.float32)
            up = up + jnp.dot(x, wu_t[k, low:high, :], preferred_element_type=jnp.float32)
            return (gate, up, square)

        carry = (
            jnp.zeros((tokens, hidden), jnp.float32),
            jnp.zeros((tokens, hidden), jnp.float32),
            jnp.zeros((tokens, 1), jnp.float32),
        )
        def forward(piece, which):
            spot = x_v[piece].at[which]
            return remote(spot, spot, fwd_ssem.at[piece], fwd_rsem.at[piece], partner)

        def own_blocks(piece, carry):
            fifteen(piece, all_ssem, all_rsem).wait_recv()
            if piece < len(PIECES) - 1:
                forward(piece, core).start()
            for b in range(SIDE):
                carry = multiply(core, b, piece, carry)
            return carry

        def partner_blocks(piece, carry):
            forward(piece, other).wait_recv()
            for b in range(SIDE):
                carry = multiply(other, b, piece, carry)
            return carry

        first = lax.rem(chip, SIDE) * (2 * req) + core * req

        def keep_rows(which, piece):
            low, high = PIECES[piece]
            line = lax.broadcasted_iota(jnp.int32, (rows, high - low), 0)
            for b in range(SIDE):
                x = x_v[piece][which, b, cy].astype(jnp.float32)
                picked = [
                    jnp.sum(jnp.where(line == first + r, x, 0.0), axis=0, keepdims=True)
                    for r in range(req)
                ]
                at = pl.multiple_of(which * half + b * block + low, LANES)
                att_ref[:, pl.ds(at, high - low)] = jnp.concatenate(picked, axis=0).astype(
                    jnp.bfloat16
                )

        for piece in range(len(PIECES)):
            fifteen(piece, red_ssem, red_rsem).wait_send()
        last = len(PIECES) - 1
        for piece in range(last + 1):
            carry = own_blocks(piece, carry)
            if piece > 0:
                carry = partner_blocks(piece - 1, carry)
                keep_rows(other, piece - 1)
            keep_rows(core, piece)
        carry = partner_blocks(last, carry)
        gate, up, square = carry
        scale = lax.rsqrt(square / width + 1e-6)
        gate = gate * scale
        up = up * scale
        mlp_ref[...] = (gate / (1.0 + jnp.exp(-gate)) * up).astype(jnp.bfloat16)

        keep_rows(other, last)

        for piece in range(len(PIECES)):
            fifteen(piece, all_ssem, red_rsem).wait_send()
        for piece in range(len(PIECES)):
            forward(piece, core).wait_send()

    return kernel


def write_out(att_ref, mlp_ref, att_hbm, mlp_hbm, sem):
    copies = (
        pltpu.make_async_copy(att_ref, att_hbm, sem.at[0]),
        pltpu.make_async_copy(mlp_ref, mlp_hbm, sem.at[1]),
    )
    for copy in copies:
        copy.start()
    for copy in copies:
        copy.wait()


def per_device(hidden_in, queries, cache, lengths, w_uv, w_out, norm_gain, w_gate, w_up):
    req, heads, depth = queries.shape
    positions = cache.shape[1]
    latent, value = w_uv.shape[1:]
    width, hidden = w_gate.shape
    rotary = depth - latent
    tokens = req * 2 * CHIPS
    half = width // 2
    block = half // SIDE
    rows = tokens // SIDE
    size = CHIPS * 16
    bf16 = jnp.bfloat16
    dma = pltpu.SemaphoreType.DMA
    hbm = pl.BlockSpec(memory_space=pltpu.HBM)
    vmem = pl.BlockSpec(memory_space=pltpu.VMEM)
    outs = (
        jax.ShapeDtypeStruct((req, width), bf16),
        jax.ShapeDtypeStruct((tokens, hidden), bf16),
    )
    att, mlp = pl.pallas_call(
        make_kernel(req, heads, latent, value, rotary, width, hidden, positions),
        out_shape=outs,
        in_specs=[hbm] * 9,
        out_specs=(vmem, vmem),
        scratch_shapes=[
            pltpu.SMEM((req,), jnp.int32),
            pltpu.VMEM((req, heads, depth), bf16),
            pltpu.VMEM((req, positions, depth), bf16),
            pltpu.VMEM((2, latent, value), bf16),
            pltpu.VMEM((2, value, half), bf16),
            pltpu.VMEM((2, req, half), bf16),
            pltpu.VMEM((width // LANES, LANES), bf16),
            pltpu.VMEM((2 * SIDE, 1, block), jnp.float32),
            pltpu.VMEM((2 * SIDE, hidden, block), bf16),
            pltpu.VMEM((2 * SIDE, hidden, block), bf16),
            pltpu.VMEM((2 * SIDE, block, hidden), bf16),
            pltpu.VMEM((2 * SIDE, block, hidden), bf16),
            pltpu.VMEM((size, size), bf16),
            pltpu.VMEM((size, size), bf16),
            pltpu.VMEM((CHIPS, 16, LANES), bf16),
            pltpu.VMEM((2 * CHIPS, 16, LANES), bf16),
            [pltpu.VMEM((SIDE, SIDE, rows, high - low), bf16) for low, high in PIECES],
            [pltpu.VMEM((CHIPS, rows, high - low), bf16) for low, high in PIECES],
            [pltpu.VMEM((2, SIDE, SIDE, rows, high - low), bf16) for low, high in PIECES],
            dma((5,)),
            dma((1,)),
            dma((1,)),
            dma((4 * SIDE,)),
            dma((1,)),
            dma((1,)),
            dma((1,)),
            dma((1,)),
            dma((1,)),
            dma((1,)),
            dma((1,)),
            dma((1,)),
            dma((len(PIECES),)),
            dma((len(PIECES),)),
            dma((len(PIECES),)),
            dma((len(PIECES),)),
            dma((len(PIECES),)),
            dma((len(PIECES),)),
        ],
        compiler_params=pltpu.CompilerParams(
            collective_id=0, has_side_effects=True, vmem_limit_bytes=40 * 1024 * 1024
        ),
    )(
        *(
            pltpu.with_memory_space_constraint(operand, pltpu.HBM)
            for operand in (
                lengths, hidden_in, queries, cache, w_uv, w_out,
                norm_gain.reshape(width // LANES, LANES), w_gate.T, w_up.T,
            )
        )
    )
    return pl.pallas_call(
        write_out,
        out_shape=outs,
        in_specs=[vmem, vmem],
        out_specs=(hbm, hbm),
        scratch_shapes=[dma((2,))],
        compiler_params=pltpu.CompilerParams(vmem_limit_bytes=1024 * 1024),
    )(att, mlp)


def solution(mesh):
    in_specs = (
        P(("group", "tp"), None),
        P(("group", "tp"), None, None),
        P(("group", "tp"), None, None),
        P(("group", "tp")),
        P("tp", None, None),
        P("tp", None),
        P(),
        P(None, "tp"),
        P(None, "tp"),
    )
    out_specs = (P(("group", "tp"), None), P("group", "tp"))
    return jax.shard_map(
        per_device, mesh=mesh, in_specs=in_specs, out_specs=out_specs, check_vma=False
    )
```
